32 devices in a mesh: groups: 2 (over x), seq: 8 (over z, y), exp: 2 (over core).
Axes of the slice: x: 2, y: 2, z: 4, core: 2. Of those that a mesh axis runs over, the one named last changes fastest.
Arguments:
- stream: bfloat16 [2048, 2048], P(('groups', 'seq', 'exp')), parts along dimension 0, may hold values from -5 to 5
- queries: bfloat16 [2048, 4096], P(('groups', 'seq'), 'exp'), parts along dimension 0, may hold values from -131 to 131
- key_rows: bfloat16 [2048, 512], P(('groups', 'seq'), 'exp'), parts along dimension 0, may hold values from -4 to 4
- value_rows: bfloat16 [2048, 512], P(('groups', 'seq'), 'exp'), parts along dimension 0, may hold values from -4 to 4
- out_weight: bfloat16 [2048, 4096], P('seq', 'exp'), may hold values from -0.375 to 0.375
- norm_gain: float32 [2048], replicated, may hold values from 0.1 to 1.9
- expert_ids: int32 [2048, 8], P(('groups', 'seq', 'exp')), parts along dimension 0, may hold values from 0 to 63, all different within a row; in each aligned block of 64 rows (0 to 63, 64 to 127, ...) at most 12 rows name the same one
- gate_weights: float32 [2048, 8], P(('groups', 'seq', 'exp')), parts along dimension 0, may hold values from 0.05 to 0.5
- expert_in: bfloat16 [64, 2048, 1536], P(('seq', 'exp')), may hold values from -0.125 to 0.125
- expert_out: bfloat16 [64, 768, 2048], P(('seq', 'exp')), may hold values from -0.21875 to 0.21875
Outputs:
- layer_out: bfloat16 [2048, 2048], P(('groups', 'seq', 'exp')), parts along dimension 0
The draws below stay inside these ranges and needn't reach their ends.
There are 2 independent parts, one for each index of `groups`. The reference program is written for one: setup_inputs(seed, part) draws one part's arguments, and reference() takes and returns one part's arrays. A program takes and returns all parts, laid end to end along the dimension named above; an argument that names none is the same for every part. Nothing has to cross between parts.
Inputs may be any that keep to these rules, and one draw needn't show every extreme that they name: `expert_ids`: each row names 8 different experts. Among the 64 rows of one device (aligned blocks of rows), no expert is named more than 12 times, a bound that some block reaches.
All inputs are finite; a program needn't handle non-finite values.
Results may differ from the reference program's by a relative error of at most 0.0095.
Values may be sent and summed in bfloat16 or wider, within the bound.
A program may use at most 128 MiB of HBM per device.

```python
import math
import jax
import jax.numpy as jnp
import numpy as np
from jax import lax

D = 2048
H = 32
KVH = 4
HD = 128
F = 768
EXPERTS = 64
TOPK = 8
CAP = 12
SPAN = 128
SEQLEN = 1024
MROWS = 64


def draw_pair(key):
    base = jax.random.fold_in(key, 7101)
    key_part, query_part = jax.random.split(base, 2)
    per_group = H // KVH
    keyed = jnp.clip(jax.random.normal(key_part, (SEQLEN, KVH, HD), jnp.float32), -3.5, 3.5)
    queried = jnp.clip(jax.random.normal(query_part, (SEQLEN, KVH, per_group, HD), jnp.float32), -3.5, 3.5)
    return (queried, keyed)


def draw_queries(key, part):
    queried, keyed = draw_pair(key)
    return queried.reshape(SEQLEN, H * HD).astype(jnp.bfloat16)


def draw_key_rows(key, part):
    queried, keyed = draw_pair(key)
    return keyed.reshape(SEQLEN, KVH * HD).astype(jnp.bfloat16)


def steps_of(key, shape, shards, least, high):
    def one(axis_at, parts):
        heights = jax.random.uniform(jax.random.fold_in(jax.random.fold_in(key, 6), axis_at), (parts,), jnp.float32, least / len(shards), high / len(shards))
        return jnp.repeat(jnp.exp(heights), shape[axis_at] // parts).reshape((-1,) + (1,) * (len(shape) - axis_at - 1))

    loudness = one(*shards[0])
    for cut in shards[1:]:
        loudness = loudness * one(*cut)
    return loudness


def assign_block(stream_key, own, number, rows, count, top, most, slope):
    sequence = jax.random.permutation(stream_key, count)
    packed, common = shares(count, rows * top, most, slope, True), shares(count, rows * top, most, slope, False)
    places = jnp.arange(count)

    def named(tallies, rotation):
        used = int((tallies > 0).sum())
        fixed = max(1, used // 4)
        passed = fixed + (places - fixed + rotation * (used - fixed)) % max(1, count - fixed)
        return jnp.zeros((count,), jnp.int32).at[sequence[jnp.where(places < fixed, places, passed)]].set(jnp.asarray(tallies, jnp.int32))

    tallies = jnp.where(number % 4 == 0, named(packed, number // 4), named(common, number - number // 4 - 1))
    mixed = jax.random.permutation(jax.random.fold_in(own, 3), count)
    giver, receiver = mixed[0:count // 2 * 2:2], mixed[1:count // 2 * 2:2]
    margin = jnp.minimum(tallies[giver] - 1, most - tallies[receiver]) // 2
    margin = jnp.where((giver == sequence[0]) | (receiver == sequence[0]) | (tallies[receiver] == 0), 0, jnp.maximum(margin, 0))
    passed = jax.random.randint(jax.random.fold_in(own, 4), (count // 2,), 0, 1 << 20) % (margin + 1)
    tallies = tallies.at[giver].add(-passed).at[receiver].add(passed)
    members = jnp.searchsorted(jnp.cumsum(tallies), jnp.arange(rows * top), side="right").astype(jnp.int32)
    listing = members.reshape(top, rows).T
    listing = listing[jax.random.permutation(jax.random.fold_in(own, 1), rows)]
    rotation = jax.random.randint(jax.random.fold_in(own, 2), (rows, 1), 0, top)
    return jnp.take_along_axis(listing, (jnp.arange(top)[None, :] + rotation) % top, axis=1)


def shares(count, total, most, lean, full):
    loads = [(1 << 20) // math.isqrt(grade ** lean) + 1 for grade in range(1, count + 1)]
    largest = most if full else min(most, max(-(-total // count), total * loads[0] // sum(loads)))
    least = 1 if total - largest >= count - 1 else 0
    holding, rest = [largest] + [least] * (count - 1), total - largest - least * (count - 1)
    while rest > 0:
        movable = [i for i in range(1, count) if holding[i] < largest] or [i for i in range(1, count) if holding[i] < most]
        pool, remaining = sum([loads[i] for i in movable]), rest
        for i in movable:
            more = min(most - holding[i], max(1, remaining * loads[i] // pool), rest)
            holding[i] = holding[i] + more
            rest = rest - more
    return np.array(holding)


def normal_values(rng, shape, deviation, most, pieces=(), held_as=jnp.bfloat16):
    result = deviation * jax.random.normal(rng, shape, jnp.float32)
    if pieces:
        result = result * steps_of(rng, shape, pieces, -0.22, 0.18)
    return jnp.clip(result, -most, most).astype(held_as)


def setup_inputs(seed: int = 0, part: int = 0) -> dict:
    key_list = jax.random.split(jax.random.key(seed), 11)
    own_keys = jax.random.split(jax.random.fold_in(key_list[10], part), 11)
    stream = normal_values(own_keys[0], (SEQLEN, D), 1.0, 5.0, ((0, 16),))
    queries = draw_queries(jax.random.fold_in(jax.random.fold_in(key_list[10], part), 71), part)
    key_rows = draw_key_rows(jax.random.fold_in(jax.random.fold_in(key_list[10], part), 71), part)
    value_rows = normal_values(own_keys[3], (SEQLEN, KVH * HD), 1.0, 4.0, ((0, 8), (1, 2)))
    out_weight = normal_values(key_list[4], (D, H * HD), (H * HD // 16) ** -0.5, 0.375, ((0, 8), (1, 2)))
    norm_gain = jnp.clip(1.0 + 0.18 * jax.random.normal(key_list[5], (D,), jnp.float32), 0.1, 1.9)
    expert_ids_keys = jax.random.split(jax.random.fold_in(own_keys[6], 1), SEQLEN // MROWS)
    expert_ids_turns = jax.random.permutation(jax.random.fold_in(own_keys[6], 3), SEQLEN // MROWS)
    expert_ids = jax.vmap(lambda own, number: assign_block(jax.random.fold_in(own_keys[6], 2), own, number, MROWS, EXPERTS, TOPK, CAP, 2))(expert_ids_keys, expert_ids_turns).reshape((SEQLEN, TOPK))
    gate_weights = jnp.clip(jnp.exp(math.log(0.5) - 2.3025851 * jax.random.uniform(own_keys[7], (SEQLEN, TOPK), jnp.float32) ** steps_of(own_keys[7], (SEQLEN, TOPK), ((0, 16),), -0.2, 0.2)), 0.05, 0.5)
    expert_in = normal_values(key_list[8], (EXPERTS, D, 2 * F), D ** -0.5, 0.125, ((0, 16),))
    expert_out = normal_values(key_list[9], (EXPERTS, F, D), F ** -0.5, 0.21875, ((0, 16),))
    return {"stream": stream, "queries": queries, "key_rows": key_rows, "value_rows": value_rows, "out_weight": out_weight, "norm_gain": norm_gain, "expert_ids": expert_ids, "gate_weights": gate_weights, "expert_in": expert_in, "expert_out": expert_out}


def attend_block(query_block, block_start, key_rows, value_rows):
    rows = query_block.shape[0]
    per_group = H // KVH
    grouped = query_block.reshape(rows, KVH, per_group, HD).astype(jnp.float32)
    keyed = key_rows.reshape(-1, KVH, HD).astype(jnp.float32)
    valued = value_rows.reshape(-1, KVH, HD).astype(jnp.float32)
    scores = jnp.einsum('tghd,sgd->gths', grouped, keyed) / jnp.sqrt(jnp.float32(HD))
    query_pos = block_start + jnp.arange(rows, dtype=jnp.int32)
    key_pos = jnp.arange(keyed.shape[0], dtype=jnp.int32)
    allowed = (key_pos[None, :] <= query_pos[:, None])[None, :, None, :]
    scores = jnp.where(allowed, scores, jnp.float32(-1e+30))
    largest = lax.optimization_barrier(jnp.max(scores, axis=-1, keepdims=True))
    exps = jnp.where(allowed, jnp.exp(scores - largest), jnp.float32(0.0))
    total = lax.optimization_barrier(jnp.sum(exps, axis=-1))
    probs = exps.astype(jnp.bfloat16)
    summed = jnp.einsum('gths,sgd->gthd', probs.astype(jnp.float32), valued)
    context = summed / total[..., None]
    return context.transpose(1, 0, 2, 3).reshape(rows, H * HD).astype(jnp.bfloat16)

def reference(stream, queries, key_rows, value_rows, out_weight, norm_gain, expert_ids, gate_weights, expert_in, expert_out):
    block_count = SEQLEN // SPAN
    blocks = queries.reshape(block_count, SPAN, H * HD)
    starts = jnp.arange(block_count, dtype=jnp.int32) * SPAN
    context = lax.map(lambda pair: attend_block(pair[0], pair[1], key_rows, value_rows), (blocks, starts))
    context = context.reshape(SEQLEN, H * HD)
    attn_out = jnp.dot(context, out_weight.T, preferred_element_type=jnp.float32)
    mixed = stream.astype(jnp.float32) + attn_out
    normed = (mixed * lax.rsqrt(lax.optimization_barrier(jnp.mean(mixed * mixed, axis=-1, keepdims=True)) + 1e-06) * norm_gain).astype(jnp.bfloat16)
    group_count = SEQLEN // MROWS
    assigned = MROWS * TOPK
    flat_ids = expert_ids.reshape(group_count, assigned)
    onehot = (flat_ids[..., None] == jnp.arange(EXPERTS, dtype=jnp.int32)[None, None, :]).astype(jnp.int32)
    earlier = jnp.cumsum(onehot, axis=1) - onehot
    slots = lax.optimization_barrier(jnp.sum(earlier * onehot, axis=-1)).astype(jnp.int32)
    group_index = jnp.arange(group_count, dtype=jnp.int32)[:, None]
    token_index = group_index * MROWS + jnp.arange(assigned, dtype=jnp.int32)[None, :] // TOPK
    position = (flat_ids * (group_count * CAP) + group_index * CAP + slots).astype(jnp.int32).reshape(-1)
    table = jnp.zeros((EXPERTS * group_count * CAP,), jnp.int32).at[position].set(token_index.reshape(-1).astype(jnp.int32))

    def run_expert(pack):
        rows_index, first, second = pack
        inputs = normed[rows_index]
        gate_up = jnp.dot(inputs, first, preferred_element_type=jnp.float32)
        act = (jax.nn.silu(gate_up[:, :F]) * gate_up[:, F:]).astype(jnp.bfloat16)
        return jnp.dot(act, second, preferred_element_type=jnp.float32).astype(jnp.bfloat16)
    results = lax.map(run_expert, (table.reshape(EXPERTS, group_count * CAP), expert_in, expert_out))
    picked = results.reshape(-1, D)[position].reshape(SEQLEN, TOPK, D)
    combined = lax.optimization_barrier(jnp.sum(gate_weights[..., None] * picked.astype(jnp.float32), axis=1))
    return (mixed + combined).astype(jnp.bfloat16)
```

```python
import functools

import jax
import jax.numpy as jnp
from jax import lax
from jax.experimental import pallas as pl
from jax.experimental.pallas import tpu as pltpu
from jax.sharding import PartitionSpec as P

HD = 128
EXPERTS = 64
CAP = 12
LOW = 2
PARTS = 4
VMEM_LIMIT = 67043328
neg_large = -1e30


def split_position():
    seq = lax.axis_index("seq")
    return seq // LOW, seq % LOW, lax.axis_index("exp")


def line_barrier(high, h, l, e):
    barrier = pltpu.get_barrier_semaphore()

    def greet(target):
        pl.semaphore_signal(barrier, inc=1, device_id=target, device_id_type=pl.DeviceIdType.MESH)

    @pl.when(h + 1 < high)
    def _():
        greet({"seq": (h + 1) * LOW + l})

    @pl.when(h > 0)
    def _():
        greet({"seq": (h - 1) * LOW + l})

    greet({"seq": h * LOW + 1 - l})
    greet({"exp": 1 - e})

    ends = jnp.where(h + 1 < high, 1, 0) + jnp.where(h > 0, 1, 0)
    pl.semaphore_wait(barrier, ends + 2)


def gather_steps(high, outs, cross, parts, recv, send, h, l, e, beside=None):
    count = len(outs)

    def slot(a, h0, l0, e0, c):
        rows = outs[a].shape[-2] // parts[a]
        at = (h0, l0, e0) if cross[a] else (h0, l0)
        return outs[a].at[at + (pl.ds(c * rows, rows),)]

    def copy(a, h0, l0, e0, c, way):
        target = (
            {"seq": (h + 1) * LOW + l},
            {"seq": (h - 1) * LOW + l},
            {"seq": h * LOW + 1 - l},
            {"exp": 1 - e},
        )[way]
        ref = slot(a, h0, l0, e0, c)
        return pltpu.make_async_remote_copy(
            src_ref=ref,
            dst_ref=ref,
            send_sem=send[a].at[way, h0, l0, c],
            recv_sem=recv[a].at[h0, l0, e0, c],
            device_id=target,
            device_id_type=pl.DeviceIdType.MESH,
        )

    def pass_on(a, h0, c, right, left):
        if right:
            @pl.when(h + 1 < high)
            def _():
                copy(a, h0, l, e, c, 0).start()
        if left:
            @pl.when(h > 0)
            def _():
                copy(a, h0, l, e, c, 1).start()
        copy(a, h0, l, e, c, 2).start()
        if cross[a]:
            copy(a, h0, l, e, c, 3).start()

    def from_across(a, h0, c):
        copy(a, h0, 1 - l, e, c, 2).wait_recv()
        if cross[a]:
            copy(a, h0, 1 - l, e, c, 3).start()

    for a in range(count):
        for c in range(parts[a]):
            pass_on(a, h, c, True, True)
    if beside is not None:
        beside(0)
    for t in range(1, high + 1):
        if t < high:
            for a in range(count):
                for c in range(parts[a]):
                    @pl.when(h - t >= 0)
                    def _():
                        copy(a, h - t, l, e, c, 0).wait_recv()
                        pass_on(a, h - t, c, True, False)

                    @pl.when(h + t < high)
                    def _():
                        copy(a, h + t, l, e, c, 1).wait_recv()
                        pass_on(a, h + t, c, False, True)
        for a in range(count):
            for c in range(parts[a]):
                if t == 1:
                    from_across(a, h, c)
                else:
                    @pl.when(h - t + 1 >= 0)
                    def _():
                        from_across(a, h - t + 1, c)

                    @pl.when(h + t - 1 < high)
                    def _():
                        from_across(a, h + t - 1, c)
        if beside is not None and t < high:
            beside(t)
    for a in range(count):
        for c in range(parts[a]):
            for h0 in range(high):
                if cross[a]:
                    for l0 in range(LOW):
                        copy(a, h0, l0, 1 - e, c, 3).wait_recv()
                        copy(a, h0, l0, e, c, 3).wait_send()
                copy(a, h0, l, e, c, 2).wait_send()

                @pl.when((h + 1 < high) & (h0 <= h))
                def _():
                    copy(a, h0, l, e, c, 0).wait_send()

                @pl.when((h > 0) & (h0 >= h))
                def _():
                    copy(a, h0, l, e, c, 1).wait_send()


def whole_barrier(seq, groups):
    barrier = pltpu.get_barrier_semaphore()
    me, e = lax.axis_index("seq"), lax.axis_index("exp")

    def greet(target):
        pl.semaphore_signal(barrier, inc=1, device_id=target, device_id_type=pl.DeviceIdType.MESH)

    greet({"exp": 1 - e})
    for d in range(1, seq):
        for e0 in range(2):
            greet({"seq": (me + d) % seq, "exp": e0})
    count = 2 * seq - 1
    if groups % 2 == 0:
        greet({"groups": flip(lax.axis_index("groups"))})
        count += 1
    pl.semaphore_wait(barrier, count)


def flip(i):
    return i + 1 - 2 * (i % 2)


def attend_piece(q, k, v, state, allowed):
    largest, total, summed = state
    scale = 1.0 / (HD ** 0.5)
    scores = lax.dot_general(
        q, k, (((1,), (1,)), ((), ())), preferred_element_type=jnp.float32
    ) * scale
    if allowed is not None:
        scores = jnp.where(allowed, scores, neg_large)
    new = jnp.maximum(largest, jnp.max(scores, axis=-1, keepdims=True))
    rescale = jnp.exp(largest - new)
    exps = jnp.exp(scores - new)
    total = total * rescale + jnp.sum(exps, axis=-1, keepdims=True)
    summed = summed * rescale + jnp.dot(
        exps.astype(jnp.bfloat16), v, preferred_element_type=jnp.float32
    )
    return new, total, summed


def front_kernel(
    high, groups, chunks, key_in, value_in, ids_ref, gates_ref, query_in, weight_in, stream_in, gain_ref,
    mixed_ref, normed_ref, meta_all,
    query_ref, stream_ref, kv, weights, contexts, part, mine, ready, landed,
    local, meta_s, meta_r, kv_s, kv_r, ctx_s, ctx_r, weight_s, weight_r, swap_s, over_s, over_r,
    away_s, away_r
):
    h, l, e = split_position()
    q, p = h // 2, h % 2
    me, seq = h * LOW + l, high * LOW
    squares = high // 2
    paired = groups % 2 == 0
    x = lax.axis_index("groups") % 2 if paired else 0
    mesh_id = pl.DeviceIdType.MESH
    heads = key_in.shape[1] // HD
    span, columns = query_ref.shape
    per_group = columns // (heads * HD)
    wide = per_group * HD
    top, rows_e = ids_ref.shape
    features = weight_in.shape[0]
    loads = []
    for g in range(heads):
        at = pl.ds(g * HD, HD)
        loads.append(pltpu.make_async_copy(key_in.at[:, at], kv.at[g, h, l, :, pl.ds(0, HD)], local.at[2 * g]))
        loads.append(pltpu.make_async_copy(value_in.at[:, at], kv.at[g, h, l, :, pl.ds(HD, HD)], local.at[2 * g + 1]))
    query_load = pltpu.make_async_copy(query_in, query_ref, local.at[2 * heads])
    weight_load = pltpu.make_async_copy(weight_in, weights.at[q], local.at[2 * heads + 1])
    stream_load = pltpu.make_async_copy(stream_in, stream_ref, local.at[2 * heads + 2])
    for one in loads + [query_load, weight_load, stream_load]:
        one.start()

    @pl.when(l == 0)
    def _():
        for g in range(heads):
            kv[g, h, 1] = jnp.zeros_like(kv[g, h, 1])

    listed = jnp.concatenate([ids_ref[...].astype(jnp.float32), gates_ref[...]], axis=0)
    blank = jnp.zeros_like(listed)
    meta_all[h, l, e] = jnp.where(
        e == 0,
        jnp.concatenate([listed, blank], axis=1),
        jnp.concatenate([blank, listed], axis=1),
    ).astype(meta_all.dtype)
    whole_barrier(seq, groups)

    def kv_copy(way, g, h0, l0):
        ref = kv.at[g, h0, l0]
        target = ({"seq": (h + 1) * LOW + l}, {"seq": h * LOW + 1 - l})[way]
        return pltpu.make_async_remote_copy(
            src_ref=ref,
            dst_ref=ref,
            send_sem=kv_s.at[way, g, h0, l0],
            recv_sem=kv_r.at[g, h0, l0],
            device_id=target,
            device_id_type=mesh_id,
        )

    def meta_copy(d, e0, source):
        s0 = (me + d) % seq
        ref = meta_all.at[h, l, e]
        return pltpu.make_async_remote_copy(
            src_ref=ref,
            dst_ref=ref,
            send_sem=meta_s.at[s0, e0],
            recv_sem=meta_r.at[source[0], source[1]],
            device_id={"seq": s0, "exp": e0},
            device_id_type=mesh_id,
        )

    def weight_rows(half, c):
        step = features // (2 * chunks)
        return pl.ds((half * chunks + c) * step, step)

    def weight_copy(q0, half, c, owner):
        ref = weights.at[owner, weight_rows(half, c)]
        return pltpu.make_async_remote_copy(
            src_ref=ref,
            dst_ref=ref,
            send_sem=weight_s.at[q0, half, c],
            recv_sem=weight_r.at[owner, half, c],
            device_id={"seq": (2 * q0 + p) * LOW + l},
            device_id_type=mesh_id,
        )

    def weight_swap(owner, half, c):
        ref = weights.at[owner, weight_rows(half, c)]
        return pltpu.make_async_remote_copy(
            src_ref=ref,
            dst_ref=ref,
            send_sem=swap_s.at[owner, c],
            recv_sem=weight_r.at[owner, half, c],
            device_id={"groups": flip(lax.axis_index("groups"))},
            device_id_type=mesh_id,
        )

    halves = [x] if paired else [0, 1]
    lower = [(d, c, half) for d in range(1, squares) for c in range(chunks) for half in halves]

    def send_weights(up, some):
        for d, c, half in some:
            q0 = (q + d) % squares

            @pl.when((q0 > q) if up else (q0 < q))
            def _():
                weight_copy(q0, half, c, q).start()

    early = [one for one in lower if one[1] < (chunks + 1) // 2]
    late = [one for one in lower if one[1] >= (chunks + 1) // 2]

    for one in loads:
        one.wait()
    for g in range(heads):
        @pl.when(h + 1 < high)
        def _():
            kv_copy(0, g, h, l).start()

        @pl.when(l == 0)
        def _():
            kv_copy(1, g, h, l).start()
    for d in range(seq):
        for e0 in range(2):
            if d > 0:
                meta_copy(d, e0, (me, e)).start()
    pltpu.make_async_remote_copy(
        src_ref=meta_all.at[h, l, e],
        dst_ref=meta_all.at[h, l, e],
        send_sem=meta_s.at[me, 1 - e],
        recv_sem=meta_r.at[me, e],
        device_id={"exp": 1 - e},
        device_id_type=mesh_id,
    ).start()
    weight_load.wait()
    send_weights(False, early)
    query_load.wait()

    def half_rows(r):
        step = span // 2
        return pl.ds(r * step, step)

    def context_copy(way, g, p0, l0, r):
        ref = contexts.at[p0, l0, g, half_rows(r)]
        target = ({"seq": (2 * q + 1 - p) * LOW + l}, {"seq": h * LOW + 1 - l})[way]
        return pltpu.make_async_remote_copy(
            src_ref=ref,
            dst_ref=ref,
            send_sem=ctx_s.at[way, g, p0, l0, r],
            recv_sem=ctx_r.at[g, p0, l0, r],
            device_id=target,
            device_id_type=mesh_id,
        )

    for g in range(heads):
        queries = jnp.concatenate(
            [query_ref[:, pl.ds((g * per_group + i) * HD, HD)] for i in range(per_group)], axis=0
        )

        def pair_of(h0):
            both = kv[g, h0].reshape(LOW * span, 2 * HD)
            return both[:, :HD], both[:, HD:]

        def across(h0):
            kv_copy(1, g, h0, 1 - l).wait_recv()

        stacked = per_group * span
        state = (
            jnp.full((stacked, 1), neg_large, jnp.float32),
            jnp.zeros((stacked, 1), jnp.float32),
            jnp.zeros((stacked, HD), jnp.float32),
        )

        @pl.when(l == 1)
        def _():
            across(h)

        k, v = pair_of(h)
        row = lax.broadcasted_iota(jnp.int32, (stacked, LOW * span), 0) % span
        column = lax.broadcasted_iota(jnp.int32, (stacked, LOW * span), 1)
        state = attend_piece(queries, k, v, state, column <= row + l * span)

        def step(t, state):
            h0 = h - t
            kv_copy(0, g, h0, l).wait_recv()

            @pl.when(h + 1 < high)
            def _():
                kv_copy(0, g, h0, l).start()

            kv_copy(1, g, h0, l).start()
            across(h0)
            k, v = pair_of(h0)
            return attend_piece(queries, k, v, state, None)

        state = lax.fori_loop(1, h + 1, step, state)
        result = (state[2] / state[1]).astype(contexts.dtype)
        for i in range(per_group):
            contexts[p, l, g, :, pl.ds(i * HD, HD)] = result[i * span : (i + 1) * span]
        for r in range(2):
            context_copy(1, g, p, l, r).start()
            context_copy(0, g, p, l, 1 - r).start()
        if g == 0:
            send_weights(False, late)
    send_weights(True, lower)

    for g in range(heads):
        for r in range(2):
            context_copy(1, g, p, 1 - l, r).wait_recv()
            if r == 0:
                context_copy(0, g, p, 1 - l, r).start()
            context_copy(0, g, 1 - p, l, 1 - r).wait_recv()
            if r == 0:
                context_copy(1, g, 1 - p, l, 1 - r).start()

    def project(d, last):
        owner = (q + d) % squares
        for i in range(2):
            l0 = l if i else 1 - l
            product = None
            for g in range(heads):
                term = lax.dot_general(
                    contexts[:, l0, g].reshape(2 * span, wide),
                    weights[owner, :, pl.ds(g * wide, wide)],
                    (((1,), (1,)), ((), ())),
                    preferred_element_type=jnp.float32,
                )
                product = term if product is None else product + term
            product = product.astype(part.dtype)
            for p0 in range(2):
                for e0 in range(2):
                    start = p0 * span + e0 * rows_e
                    part[p0, l0, e0, owner] = product[start : start + rows_e]
            if last:
                for p0 in range(2):
                    over(p0, l0).start()

    def over(p0, l0):
        return pltpu.make_async_remote_copy(
            src_ref=part.at[p0, l0, 1 - e],
            dst_ref=mine.at[p0, l0],
            send_sem=over_s.at[p0, l0],
            recv_sem=over_r.at[p0, l0],
            device_id={"exp": 1 - e},
            device_id_type=mesh_id,
        )

    def forward(some):
        for d, c, half in some:
            owner = (q + d) % squares
            weight_copy(owner, half, c, owner).wait_recv()
            if paired:
                weight_swap(owner, half, c).start()

    split = max(1, len(lower) * 3 // 4) if lower else 0
    forward(lower[:split])
    for g in range(heads):
        context_copy(0, g, 1 - p, 1 - l, 0).wait_recv()
        context_copy(1, g, 1 - p, 1 - l, 1).wait_recv()
    project(0, squares == 1)
    forward(lower[split:])
    for d in range(1, squares):
        for c in range(chunks):
            if paired:
                weight_swap((q + d) % squares, 1 - x, c).wait_recv()
        project(d, d == squares - 1)

    def away(p0, l0, p1, l1):
        return pltpu.make_async_remote_copy(
            src_ref=ready.at[p0, l0],
            dst_ref=landed.at[p1, l1],
            send_sem=away_s.at[p0, l0],
            recv_sem=away_r.at[p1, l1],
            device_id={"seq": (2 * q + p0) * LOW + l0},
            device_id_type=mesh_id,
        )

    others = ((1 - p, 1 - l), (p, 1 - l), (1 - p, l))
    for p0, l0 in others + ((p, l),):
        over(p0, l0).wait_recv()
    for p0, l0 in others:
        total = part[p0, l0, e].astype(jnp.float32) + mine[p0, l0].astype(jnp.float32)
        ready[p0, l0] = total.astype(ready.dtype)
        away(p0, l0, p, l).start()
    landed[p, l] = (part[p, l, e].astype(jnp.float32) + mine[p, l].astype(jnp.float32)).astype(landed.dtype)
    stream_load.wait()
    for p0, l0 in others:
        away(p0, l0, p0, l0).wait_recv()
    squared = None
    for h0 in range(high):
        block = pl.ds(h0 * LOW * features, LOW * features)
        pair = jnp.concatenate([landed[h0 % 2, l0, h0 // 2] for l0 in range(LOW)], axis=1)
        value = stream_ref[:, block].astype(jnp.float32) + pair.astype(jnp.float32)
        mixed_ref[:, block] = value
        term = jnp.sum(value * value, axis=-1, keepdims=True)
        squared = term if squared is None else squared + term
    factor = lax.rsqrt(squared / (high * LOW * features) + 1e-06)
    for h0 in range(high):
        block = pl.ds(h0 * LOW * features, LOW * features)
        normed_ref[:, block] = (mixed_ref[:, block] * factor * gain_ref[:, block]).astype(
            normed_ref.dtype
        )

    for d in range(seq):
        for e0 in range(2):
            if d > 0:
                meta_copy(d, e0, ((me + d) % seq, e0)).wait_recv()
                meta_copy(d, e0, (me, e)).wait_send()
    peer = pltpu.make_async_remote_copy(
        src_ref=meta_all.at[h, l, e],
        dst_ref=meta_all.at[h, l, e],
        send_sem=meta_s.at[me, 1 - e],
        recv_sem=meta_r.at[me, 1 - e],
        device_id={"exp": 1 - e},
        device_id_type=mesh_id,
    )
    peer.wait_recv()
    peer.wait_send()
    for g in range(heads):
        @pl.when(h + 1 < high)
        def _():
            kv_copy(0, g, h, l).wait_send()

        @pl.when(l == 0)
        def _():
            kv_copy(1, g, h, l).wait_send()

        @pl.loop(1, h + 1)
        def _(t):
            @pl.when(h + 1 < high)
            def _():
                kv_copy(0, g, h - t, l).wait_send()

            kv_copy(1, g, h - t, l).wait_send()

        for way in range(2):
            for r in range(2):
                context_copy(way, g, p, l, r).wait_send()
        context_copy(0, g, p, 1 - l, 0).wait_send()
        context_copy(1, g, 1 - p, l, 1).wait_send()
    for d, c, half in lower:
        weight_copy((q + d) % squares, half, c, q).wait_send()
        if paired:
            weight_swap((q + d) % squares, half, c).wait_send()
    for p0, l0 in others:
        away(p0, l0, p, l).wait_send()
    for p0, l0 in others + ((p, l),):
        over(p0, l0).wait_send()


def front(keys, values, ids, gates, queries, weight, stream, gain, high, groups):
    whole = pl.BlockSpec(memory_space=pltpu.VMEM)
    away = pl.BlockSpec(memory_space=pl.ANY)
    span, columns = queries.shape
    rows = stream.shape[0]
    features = weight.shape[0]
    heads = keys.shape[1] // HD
    squares = high // 2
    chunks = 4 if features % 128 == 0 else 1
    kind = jnp.bfloat16
    sem = pltpu.SemaphoreType.DMA
    return pl.pallas_call(
        functools.partial(front_kernel, high, groups, chunks),
        out_shape=(
            jax.ShapeDtypeStruct(stream.shape, jnp.float32),
            jax.ShapeDtypeStruct(stream.shape, kind),
            jax.ShapeDtypeStruct((high, LOW, 2, 2 * ids.shape[0], 2 * rows), kind),
        ),
        in_specs=[away, away, whole, whole, away, away, away, whole],
        out_specs=(whole,) * 3,
        scratch_shapes=[
            pltpu.VMEM(queries.shape, kind),
            pltpu.VMEM(stream.shape, kind),
            pltpu.VMEM((heads, high, LOW, span, 2 * HD), kind),
            pltpu.VMEM((squares,) + weight.shape, kind),
            pltpu.VMEM((2, LOW, heads, span, columns // heads), kind),
            pltpu.VMEM((2, LOW, 2, squares, rows, features), kind),
            pltpu.VMEM((2, LOW, squares, rows, features), kind),
            pltpu.VMEM((2, LOW, squares, rows, features), kind),
            pltpu.VMEM((2, LOW, squares, rows, features), kind),
            sem((2 * heads + 3,)),
            sem((high * LOW, 2)),
            sem((high * LOW, 2)),
            sem((2, heads, high, LOW)),
            sem((heads, high, LOW)),
            sem((2, heads, 2, LOW, 2)),
            sem((heads, 2, LOW, 2)),
            sem((squares, 2, chunks)),
            sem((squares, 2, chunks)),
            sem((squares, chunks)),
            sem((2, LOW)),
            sem((2, LOW)),
            sem((2, LOW)),
            sem((2, LOW)),
        ],
        compiler_params=pltpu.CompilerParams(
            collective_id=1, has_side_effects=True, vmem_limit_bytes=VMEM_LIMIT
        ),
        name="front",
    )(keys, values, ids, gates, queries, weight, stream, gain)


def back_kernel(
    high, parts, top, normed_ref, mixed_ref, meta_ref, first_hbm, second_hbm, out_ref,
    choose_ref, combine_ref, every, first, second, picked, act, near, sums, across, running, line,
    local, weight_sem, recv, send, near_s, near_r, across_s, across_r, line_s, line_r
):
    h, l, e = split_position()
    experts, width, double = first.shape
    hidden = double // 2
    slots = picked.shape[2]
    loads = []
    for i in range(experts):
        loads.append(pltpu.make_async_copy(first_hbm.at[i], first.at[i], weight_sem.at[0, i]))
        loads.append(pltpu.make_async_copy(second_hbm.at[i], second.at[i], weight_sem.at[1, i]))
    for one in loads:
        one.start()
    own = pltpu.make_async_copy(normed_ref, every.at[h, l, e], local.at[0])
    own.start()
    line_barrier(high, h, l, e)
    own.wait()
    device = (h * LOW + l) * 2 + e
    tokens_here, total = combine_ref.shape[1:]
    span = every.shape[3]

    def build(h0):
        meta = jnp.concatenate(
            [
                meta_ref[h0, l0, 0].astype(jnp.float32) + meta_ref[h0, l0, 1].astype(jnp.float32)
                for l0 in range(LOW)
            ],
            axis=1,
        )
        ids, gates = meta[:top], meta[top:]
        chosen, shares = [], []
        for i in range(experts):
            hit = ids == (device * experts + i).astype(jnp.float32)
            chosen.append(jnp.sum(jnp.where(hit, 1.0, 0.0), axis=0, keepdims=True))
            shares.append(jnp.sum(jnp.where(hit, gates, 0.0), axis=0, keepdims=True))
        line_up = jnp.concatenate(
            chosen + [jnp.zeros_like(chosen[0])] * (-experts % 8), axis=0
        )
        square = (tokens_here, tokens_here)
        row = lax.broadcasted_iota(jnp.int32, square, 0)
        column = lax.broadcasted_iota(jnp.int32, square, 1)
        earlier = jnp.where((row < column) & (row // span == column // span), 1.0, 0.0)
        place = jnp.dot(
            line_up.astype(jnp.bfloat16), earlier.astype(jnp.bfloat16), preferred_element_type=jnp.float32
        )
        tall = (-(-total // 128) * 128, tokens_here)
        number = lax.broadcasted_iota(jnp.int32, tall, 0).astype(jnp.float32)
        block = (lax.broadcasted_iota(jnp.int32, (1, tokens_here), 1) // span).astype(jnp.float32)
        onehot, weigh = jnp.zeros(tall, jnp.float32), jnp.zeros(tall, jnp.float32)
        for i in range(experts):
            match = (number == place[i : i + 1] + block * CAP + i * slots) & (chosen[i] > 0.5)
            onehot = onehot + jnp.where(match, 1.0, 0.0)
            weigh = weigh + jnp.where(match, shares[i], 0.0)
        choose_ref[h0] = onehot[:total].astype(choose_ref.dtype)
        combine_ref[h0] = jnp.transpose(weigh)[:, :total].astype(combine_ref.dtype)

    gather_steps(high, (every,), (True,), (parts,), (recv,), (send,), h, l, e, build)
    for one in loads:
        one.wait()
    rows_all = every.shape[1] * every.shape[2] * every.shape[3]
    tile = 512

    @pl.loop(0, high)
    def _(h0):
        for n in range(0, width, tile):
            tokens = every[h0, :, :, :, pl.ds(n, tile)].reshape(rows_all, tile)
            value = jnp.dot(choose_ref[h0], tokens, preferred_element_type=jnp.float32)
            for i in range(experts):
                picked[i, h0, :, pl.ds(n, tile)] = value[i * slots : (i + 1) * slots].astype(
                    picked.dtype
                )

    def run(i, carry):
        step = 256
        rows = picked[i].reshape(high * slots, width)
        for f in range(0, hidden, step):
            gate = jnp.dot(rows, first[i, :, pl.ds(f, step)], preferred_element_type=jnp.float32)
            up = jnp.dot(
                rows, first[i, :, pl.ds(hidden + f, step)], preferred_element_type=jnp.float32
            )
            act[:, pl.ds(f, step)] = (gate / (1.0 + jnp.exp(-gate)) * up).astype(act.dtype)
        for n in range(0, width, tile):
            value = jnp.dot(
                act[...], second[i, :, pl.ds(n, tile)], preferred_element_type=jnp.float32
            ).astype(picked.dtype)
            picked[i, :, :, pl.ds(n, tile)] = value.reshape(high, slots, tile)
        return carry

    lax.fori_loop(0, experts, run, 0)
    scatter_steps(
        high, parts, every, mixed_ref, out_ref, near, sums, across, running, line,
        near_s, near_r, across_s, across_r, line_s, line_r, h, l, e, combine_ref, picked, tile
    )


def scatter_steps(
    high, parts, part_ref, mixed_ref, out_ref, near, sums, across, running, line,
    near_s, near_r, across_s, across_r, line_s, line_r, h, l, e, combine_ref, picked, tile
):
    rows = part_ref.shape[-2] // parts
    mesh_id = pl.DeviceIdType.MESH
    order = []
    for i in range(high):
        order.append(i // 2 if i % 2 == 0 else high - 1 - i // 2)

    def to_near(h0, l0, c):
        at = pl.ds(c * rows, rows)
        return pltpu.make_async_remote_copy(
            src_ref=part_ref.at[h0, l0, 1 - e, at],
            dst_ref=near.at[h0, l0, at],
            send_sem=near_s.at[h0, l0, c],
            recv_sem=near_r.at[h0, l0, c],
            device_id={"exp": 1 - e},
            device_id_type=mesh_id,
        )

    def to_across(h0, c):
        at = pl.ds(c * rows, rows)
        return pltpu.make_async_remote_copy(
            src_ref=sums.at[h0, at],
            dst_ref=across.at[h0, at],
            send_sem=across_s.at[h0, c],
            recv_sem=across_r.at[h0, c],
            device_id={"seq": h * LOW + 1 - l},
            device_id_type=mesh_id,
        )

    def to_line(way, h0, c):
        at = pl.ds(c * rows, rows)
        return pltpu.make_async_remote_copy(
            src_ref=running.at[h0, at],
            dst_ref=line.at[way, h0, at],
            send_sem=line_s.at[way, h0, c],
            recv_sem=line_r.at[way, h0, c],
            device_id={"seq": (h - 1 + 2 * way) * LOW + l},
            device_id_type=mesh_id,
        )

    pieces = [(h0, c) for h0 in order for c in range(parts)]
    experts, width = picked.shape[0], picked.shape[-1]
    shape = part_ref.shape[1:4]
    for h0 in order:
        for n in range(0, width, tile):
            rows_here = jnp.concatenate(
                [picked[i, h0, :, pl.ds(n, tile)] for i in range(experts)], axis=0
            )
            value = jnp.dot(combine_ref[h0], rows_here, preferred_element_type=jnp.float32)
            part_ref[h0, :, :, :, pl.ds(n, tile)] = value.astype(part_ref.dtype).reshape(
                shape + (tile,)
            )
        for c in range(parts):
            to_near(h0, 1 - l, c).start()
        for c in range(parts):
            to_near(h0, l, c).start()
    for h0, c in pieces:
        at = pl.ds(c * rows, rows)
        to_near(h0, 1 - l, c).wait_recv()
        value = part_ref[h0, 1 - l, e, at].astype(jnp.float32) + near[h0, 1 - l, at].astype(jnp.float32)
        sums[h0, at] = value.astype(sums.dtype)
        to_across(h0, c).start()
    for h0, c in pieces:
        at = pl.ds(c * rows, rows)
        to_near(h0, l, c).wait_recv()
        to_across(h0, c).wait_recv()

        def held():
            value = part_ref[h0, l, e, at].astype(jnp.float32) + near[h0, l, at].astype(jnp.float32)
            return value + across[h0, at].astype(jnp.float32)

        @pl.when(h0 < h)
        def _():
            @pl.when(h + 1 < high)
            def _():
                to_line(0, h0, c).wait_recv()
                running[h0, at] = (held() + line[0, h0, at].astype(jnp.float32)).astype(running.dtype)

            @pl.when(h + 1 >= high)
            def _():
                running[h0, at] = held().astype(running.dtype)

            to_line(0, h0, c).start()

        @pl.when(h0 > h)
        def _():
            @pl.when(h > 0)
            def _():
                to_line(1, h0, c).wait_recv()
                running[h0, at] = (held() + line[1, h0, at].astype(jnp.float32)).astype(running.dtype)

            @pl.when(h <= 0)
            def _():
                running[h0, at] = held().astype(running.dtype)

            to_line(1, h0, c).start()
    for c in range(parts):
        at = pl.ds(c * rows, rows)
        value = part_ref[h, l, e, at].astype(jnp.float32) + near[h, l, at].astype(jnp.float32)
        value = value + across[h, at].astype(jnp.float32) + mixed_ref[at, :]
        mixed_ref_sum = value

        @pl.when(h + 1 < high)
        def _():
            to_line(0, h, c).wait_recv()

        @pl.when(h + 1 >= high)
        def _():
            line[0, h, at] = jnp.zeros_like(line[0, h, at])

        @pl.when(h > 0)
        def _():
            to_line(1, h, c).wait_recv()

        @pl.when(h <= 0)
        def _():
            line[1, h, at] = jnp.zeros_like(line[1, h, at])

        value = mixed_ref_sum + line[0, h, at].astype(jnp.float32) + line[1, h, at].astype(jnp.float32)
        out_ref[at, :] = value.astype(out_ref.dtype)
    for h0, c in pieces:
        to_near(h0, l, c).wait_send()
        to_near(h0, 1 - l, c).wait_send()
        to_across(h0, c).wait_send()

        @pl.when(h0 < h)
        def _():
            to_line(0, h0, c).wait_send()

        @pl.when(h0 > h)
        def _():
            to_line(1, h0, c).wait_send()


def back(normed, mixed, meta, expert_in, expert_out, high, top):
    rows, width = mixed.shape
    parts = PARTS
    whole = pl.BlockSpec(memory_space=pltpu.VMEM)
    away = pl.BlockSpec(memory_space=pl.ANY)
    kind = jnp.bfloat16
    sem = pltpu.SemaphoreType.DMA
    experts = expert_in.shape[0]
    slots = LOW * 2 * CAP
    tokens = LOW * 2 * rows
    return pl.pallas_call(
        functools.partial(back_kernel, high, parts, top),
        out_shape=jax.ShapeDtypeStruct((rows, width), kind),
        in_specs=[whole] * 3 + [away] * 2,
        out_specs=whole,
        scratch_shapes=[
            pltpu.VMEM((high, experts * slots, tokens), kind),
            pltpu.VMEM((high, tokens, experts * slots), kind),
            pltpu.VMEM((high, LOW, 2, rows, width), kind),
            pltpu.VMEM(expert_in.shape, kind),
            pltpu.VMEM(expert_out.shape, kind),
            pltpu.VMEM((experts, high, slots, width), kind),
            pltpu.VMEM((high * slots, expert_out.shape[1]), kind),
            pltpu.VMEM((high, LOW, rows, width), kind),
            pltpu.VMEM((high, rows, width), kind),
            pltpu.VMEM((high, rows, width), kind),
            pltpu.VMEM((high, rows, width), kind),
            pltpu.VMEM((2, high, rows, width), kind),
            sem((1,)),
            sem((2, experts)),
            sem((high, LOW, 2, parts)),
            sem((4, high, LOW, parts)),
        ]
        + [sem((high, LOW, parts))] * 2
        + [sem((high, parts))] * 2
        + [sem((2, high, parts))] * 2,
        compiler_params=pltpu.CompilerParams(
            collective_id=2, has_side_effects=True, vmem_limit_bytes=VMEM_LIMIT
        ),
        name="back",
    )(normed, mixed, meta, expert_in, expert_out)


def on_device(
    stream,
    queries,
    key_rows,
    value_rows,
    out_weight,
    norm_gain,
    expert_ids,
    gate_weights,
    expert_in,
    expert_out,
):
    high = lax.axis_size("seq") // LOW
    mixed, normed, meta = front(
        key_rows, value_rows, expert_ids.T, gate_weights.T, queries, out_weight, stream,
        norm_gain.reshape(1, -1), high, lax.axis_size("groups"),
    )
    return back(normed, mixed, meta, expert_in, expert_out, high, expert_ids.shape[1])


def solution(mesh):
    in_specs = (
        P(("groups", "seq", "exp"), None),
        P(("groups", "seq"), "exp"),
        P(("groups", "seq"), "exp"),
        P(("groups", "seq"), "exp"),
        P("seq", "exp"),
        P(),
        P(("groups", "seq", "exp"), None),
        P(("groups", "seq", "exp"), None),
        P(("seq", "exp"), None, None),
        P(("seq", "exp"), None, None),
    )
    out_specs = P(("groups", "seq", "exp"), None)
    return jax.shard_map(
        on_device, mesh=mesh, in_specs=in_specs, out_specs=out_specs, check_vma=False
    )
```

```python
import functools

import jax
import jax.numpy as jnp
from jax import lax
from jax.experimental import pallas as pl
from jax.experimental.pallas import tpu as pltpu
from jax.sharding import PartitionSpec as P

HD = 128
EXPERTS = 64
CAP = 12
LOW = 2
PARTS = 4
VMEM_LIMIT = 67043328
neg_large = -1e30


def split_position():
    seq = lax.axis_index("seq")
    return seq // LOW, seq % LOW, lax.axis_index("exp")


def line_barrier(high, h, l, e):
    barrier = pltpu.get_barrier_semaphore()

    def greet(target):
        pl.semaphore_signal(barrier, inc=1, device_id=target, device_id_type=pl.DeviceIdType.MESH)

    @pl.when(h + 1 < high)
    def _():
        greet({"seq": (h + 1) * LOW + l})

    @pl.when(h > 0)
    def _():
        greet({"seq": (h - 1) * LOW + l})

    greet({"seq": h * LOW + 1 - l})
    greet({"exp": 1 - e})

    ends = jnp.where(h + 1 < high, 1, 0) + jnp.where(h > 0, 1, 0)
    pl.semaphore_wait(barrier, ends + 2)


def whole_barrier(seq, groups):
    barrier = pltpu.get_barrier_semaphore()
    me, e = lax.axis_index("seq"), lax.axis_index("exp")

    def greet(target):
        pl.semaphore_signal(barrier, inc=1, device_id=target, device_id_type=pl.DeviceIdType.MESH)

    greet({"exp": 1 - e})
    for d in range(1, seq):
        for e0 in range(2):
            greet({"seq": (me + d) % seq, "exp": e0})
    count = 2 * seq - 1
    if groups % 2 == 0:
        greet({"groups": flip(lax.axis_index("groups"))})
        count += 1
    pl.semaphore_wait(barrier, count)


def flip(i):
    return i + 1 - 2 * (i % 2)


def attend_piece(q, k, v, state, allowed):
    largest, total, summed = state
    scale = 1.0 / (HD ** 0.5)
    scores = lax.dot_general(
        q, k, (((1,), (1,)), ((), ())), preferred_element_type=jnp.float32
    ) * scale
    if allowed is not None:
        scores = jnp.where(allowed, scores, neg_large)
    new = jnp.maximum(largest, jnp.max(scores, axis=-1, keepdims=True))
    rescale = jnp.exp(largest - new)
    exps = jnp.exp(scores - new)
    total = total * rescale + jnp.sum(exps, axis=-1, keepdims=True)
    summed = summed * rescale + jnp.dot(
        exps.astype(jnp.bfloat16), v, preferred_element_type=jnp.float32
    )
    return new, total, summed


def front_kernel(
    high, groups, chunks, key_in, value_in, ids_ref, gates_ref, query_in, weight_in, stream_in, gain_ref,
    mixed_ref, normed_ref, meta_all,
    query_ref, stream_ref, kv, weights, contexts, part, mine, ready, landed,
    local, meta_s, meta_r, kv_s, kv_r, ctx_s, ctx_r, weight_s, weight_r, swap_s, over_s, over_r,
    away_s, away_r, turn
):
    h, l, e = split_position()
    q, p = h // 2, h % 2
    me, seq = h * LOW + l, high * LOW
    squares = high // 2
    paired = groups % 2 == 0
    x = lax.axis_index("groups") % 2 if paired else 0
    mesh_id = pl.DeviceIdType.MESH
    heads = key_in.shape[1] // HD
    span, columns = query_ref.shape
    per_group = columns // (heads * HD)
    wide = per_group * HD
    top, rows_e = ids_ref.shape
    features = weight_in.shape[0]
    loads = []
    for g in range(heads):
        at = pl.ds(g * HD, HD)
        loads.append(pltpu.make_async_copy(key_in.at[:, at], kv.at[g, h, l, :, pl.ds(0, HD)], local.at[2 * g]))
        loads.append(pltpu.make_async_copy(value_in.at[:, at], kv.at[g, h, l, :, pl.ds(HD, HD)], local.at[2 * g + 1]))
    query_load = pltpu.make_async_copy(query_in, query_ref, local.at[2 * heads])
    weight_load = pltpu.make_async_copy(weight_in, weights.at[q], local.at[2 * heads + 1])
    stream_load = pltpu.make_async_copy(stream_in, stream_ref, local.at[2 * heads + 2])
    for one in loads + [query_load, weight_load, stream_load]:
        one.start()

    @pl.when(l == 0)
    def _():
        for g in range(heads):
            kv[g, h, 1] = jnp.zeros_like(kv[g, h, 1])

    listed = jnp.concatenate([ids_ref[...].astype(jnp.float32), gates_ref[...]], axis=0)
    blank = jnp.zeros_like(listed)
    meta_all[h, l, e] = jnp.where(
        l == 0,
        jnp.concatenate([listed, blank], axis=1),
        jnp.concatenate([blank, listed], axis=1),
    ).astype(meta_all.dtype)
    whole_barrier(seq, groups)

    def kv_copy(way, g, h0, l0):
        ref = kv.at[g, h0, l0]
        target = ({"seq": (h + 1) * LOW + l}, {"seq": h * LOW + 1 - l})[way]
        return pltpu.make_async_remote_copy(
            src_ref=ref,
            dst_ref=ref,
            send_sem=kv_s.at[way, g, h0, l0],
            recv_sem=kv_r.at[g, h0, l0],
            device_id=target,
            device_id_type=mesh_id,
        )

    def meta_copy(d, e0, source):
        s0 = (me + d) % seq
        ref = meta_all.at[h, l, e]
        return pltpu.make_async_remote_copy(
            src_ref=ref,
            dst_ref=ref,
            send_sem=meta_s.at[s0, e0],
            recv_sem=meta_r.at[source[0], source[1]],
            device_id={"seq": s0, "exp": e0},
            device_id_type=mesh_id,
        )

    def weight_rows(half, c):
        step = features // (2 * chunks)
        return pl.ds((half * chunks + c) * step, step)

    def weight_copy(q0, half, c, owner):
        ref = weights.at[owner, weight_rows(half, c)]
        return pltpu.make_async_remote_copy(
            src_ref=ref,
            dst_ref=ref,
            send_sem=weight_s.at[q0, half, c],
            recv_sem=weight_r.at[owner, half, c],
            device_id={"seq": (2 * q0 + p) * LOW + l},
            device_id_type=mesh_id,
        )

    def weight_swap(owner, half, c):
        ref = weights.at[owner, weight_rows(half, c)]
        return pltpu.make_async_remote_copy(
            src_ref=ref,
            dst_ref=ref,
            send_sem=swap_s.at[owner, c],
            recv_sem=weight_r.at[owner, half, c],
            device_id={"groups": flip(lax.axis_index("groups"))},
            device_id_type=mesh_id,
        )

    halves = [x] if paired else [0, 1]
    lower = [(d, c, half) for d in range(1, squares) for c in range(chunks) for half in halves]

    def send_weights(up):
        for d, c, half in lower:
            q0 = (q + d) % squares

            @pl.when((q0 > q) if up else (q0 < q))
            def _():
                weight_copy(q0, half, c, q).start()

    for one in loads:
        one.wait()
    for g in range(heads):
        @pl.when(h + 1 < high)
        def _():
            kv_copy(0, g, h, l).start()

        @pl.when(l == 0)
        def _():
            kv_copy(1, g, h, l).start()
    for d in range(seq):
        for e0 in range(2):
            if d > 0:
                meta_copy(d, e0, (me, e)).start()
    pltpu.make_async_remote_copy(
        src_ref=meta_all.at[h, l, e],
        dst_ref=meta_all.at[h, l, e],
        send_sem=meta_s.at[me, 1 - e],
        recv_sem=meta_r.at[me, e],
        device_id={"exp": 1 - e},
        device_id_type=mesh_id,
    ).start()
    weight_load.wait()
    @pl.when(p == 0)
    def _():
        send_weights(False)

    query_load.wait()

    def half_rows(r):
        step = span // 2
        return pl.ds(r * step, step)

    def context_copy(way, g, p0, l0, r):
        ref = contexts.at[p0, l0, g, half_rows(r)]
        target = ({"seq": (2 * q + 1 - p) * LOW + l}, {"seq": h * LOW + 1 - l})[way]
        return pltpu.make_async_remote_copy(
            src_ref=ref,
            dst_ref=ref,
            send_sem=ctx_s.at[way, g, p0, l0, r],
            recv_sem=ctx_r.at[g, p0, l0, r],
            device_id=target,
            device_id_type=mesh_id,
        )

    queries = [
        jnp.concatenate(
            [query_ref[:, pl.ds((g * per_group + i) * HD, HD)] for i in range(per_group)], axis=0
        )
        for g in range(heads)
    ]

    def attend(h0, states, allowed):
        result = []
        for g in range(heads):
            both = kv[g, h0].reshape(LOW * span, 2 * HD)
            result.append(attend_piece(queries[g], both[:, :HD], both[:, HD:], states[g], allowed))
        return tuple(result)

    def across(h0):
        for g in range(heads):
            kv_copy(1, g, h0, 1 - l).wait_recv()

    def relay(h0):
        for g in range(heads):
            kv_copy(0, g, h0, l).wait_recv()

            @pl.when(h + 1 < high)
            def _():
                kv_copy(0, g, h0, l).start()

            kv_copy(1, g, h0, l).start()

    @pl.when(h > 0)
    def _():
        relay(h - 1)

    @pl.when(l == 1)
    def _():
        across(h)

    stacked = per_group * span
    states = tuple(
        (
            jnp.full((stacked, 1), neg_large, jnp.float32),
            jnp.zeros((stacked, 1), jnp.float32),
            jnp.zeros((stacked, HD), jnp.float32),
        )
        for _ in range(heads)
    )
    row = lax.broadcasted_iota(jnp.int32, (stacked, LOW * span), 0) % span
    column = lax.broadcasted_iota(jnp.int32, (stacked, LOW * span), 1)
    states = attend(h, states, column <= row + l * span)

    def step(t, states):
        @pl.when(t < h)
        def _():
            relay(h - t - 1)

        @pl.when((t == 1) & (p == 1))
        def _():
            send_weights(False)

        across(h - t)
        return attend(h - t, states, None)

    states = lax.fori_loop(1, h + 1, step, states)
    for g in range(heads):
        @pl.when(l == 0)
        def _():
            kv_copy(1, g, h, l).wait_send()

        @pl.loop(1, h + 1)
        def _(t):
            kv_copy(1, g, h - t, l).wait_send()

    pl.semaphore_signal(turn, inc=1, device_id={"exp": 1 - e}, device_id_type=mesh_id)
    pl.semaphore_wait(turn, 1)
    for g in range(heads):
        result = (states[g][2] / states[g][1]).astype(contexts.dtype)
        for i in range(per_group):
            contexts[p, l, g, :, pl.ds(i * HD, HD)] = result[i * span : (i + 1) * span]
        for r in range(2):
            context_copy(1, g, p, l, r).start()
            context_copy(0, g, p, l, 1 - r).start()

    send_weights(True)

    def pass_contexts(g):
        for r in range(2):
            context_copy(1, g, p, 1 - l, r).wait_recv()
            if r == 0 and g == 0:
                context_copy(0, g, p, 1 - l, r).start()
            elif r == 0:
                @pl.when(p == 1)
                def _():
                    context_copy(0, g, p, 1 - l, r).start()

            context_copy(0, g, 1 - p, l, 1 - r).wait_recv()
            if r == 0:
                context_copy(1, g, 1 - p, l, 1 - r).start()
            elif g > 0:
                @pl.when(p == 1)
                def _():
                    context_copy(1, g, 1 - p, l, 1 - r).start()

    def project(d, last):
        owner = (q + d) % squares
        for i in range(2):
            l0 = l if i else 1 - l
            product = None
            for g in range(heads):
                term = lax.dot_general(
                    contexts[:, l0, g].reshape(2 * span, wide),
                    weights[owner, :, pl.ds(g * wide, wide)],
                    (((1,), (1,)), ((), ())),
                    preferred_element_type=jnp.float32,
                )
                product = term if product is None else product + term
            product = product.astype(part.dtype)
            for p0 in range(2):
                for e0 in range(2):
                    start = p0 * span + e0 * rows_e
                    part[p0, l0, e0, owner] = product[start : start + rows_e]
            if last:
                for p0 in range(2):
                    over(p0, l0).start()

    def over(p0, l0):
        return pltpu.make_async_remote_copy(
            src_ref=part.at[p0, l0, 1 - e],
            dst_ref=mine.at[p0, l0],
            send_sem=over_s.at[p0, l0],
            recv_sem=over_r.at[p0, l0],
            device_id={"exp": 1 - e},
            device_id_type=mesh_id,
        )

    def forward(some):
        for d, c, half in some:
            owner = (q + d) % squares
            weight_copy(owner, half, c, owner).wait_recv()
            if paired:
                weight_swap(owner, half, c).start()

    split = len(lower) // 2
    for g in range(heads):
        pass_contexts(g)
        forward(lower[:split] if g == 0 else lower[split:])
    for g in range(heads):
        context_copy(0, g, 1 - p, 1 - l, 0).wait_recv()
        context_copy(1, g, 1 - p, 1 - l, 1).wait_recv()
    project(0, squares == 1)
    for d in range(1, squares):
        for c in range(chunks):
            if paired:
                weight_swap((q + d) % squares, 1 - x, c).wait_recv()
        project(d, d == squares - 1)

    def away(p0, l0, p1, l1):
        return pltpu.make_async_remote_copy(
            src_ref=ready.at[p0, l0],
            dst_ref=landed.at[p1, l1],
            send_sem=away_s.at[p0, l0],
            recv_sem=away_r.at[p1, l1],
            device_id={"seq": (2 * q + p0) * LOW + l0},
            device_id_type=mesh_id,
        )

    others = ((1 - p, 1 - l), (p, 1 - l), (1 - p, l))
    for p0, l0 in others + ((p, l),):
        over(p0, l0).wait_recv()
    for p0, l0 in others:
        total = part[p0, l0, e].astype(jnp.float32) + mine[p0, l0].astype(jnp.float32)
        ready[p0, l0] = total.astype(ready.dtype)
        away(p0, l0, p, l).start()
    landed[p, l] = (part[p, l, e].astype(jnp.float32) + mine[p, l].astype(jnp.float32)).astype(landed.dtype)
    stream_load.wait()
    for p0, l0 in others:
        away(p0, l0, p0, l0).wait_recv()
    squared = None
    for h0 in range(high):
        block = pl.ds(h0 * LOW * features, LOW * features)
        pair = jnp.concatenate([landed[h0 % 2, l0, h0 // 2] for l0 in range(LOW)], axis=1)
        value = stream_ref[:, block].astype(jnp.float32) + pair.astype(jnp.float32)
        mixed_ref[:, block] = value
        term = jnp.sum(value * value, axis=-1, keepdims=True)
        squared = term if squared is None else squared + term
    factor = lax.rsqrt(squared / (high * LOW * features) + 1e-06)
    for h0 in range(high):
        block = pl.ds(h0 * LOW * features, LOW * features)
        normed_ref[:, block] = (mixed_ref[:, block] * factor * gain_ref[:, block]).astype(
            normed_ref.dtype
        )

    for d in range(seq):
        for e0 in range(2):
            if d > 0:
                meta_copy(d, e0, ((me + d) % seq, e0)).wait_recv()
                meta_copy(d, e0, (me, e)).wait_send()
    peer = pltpu.make_async_remote_copy(
        src_ref=meta_all.at[h, l, e],
        dst_ref=meta_all.at[h, l, e],
        send_sem=meta_s.at[me, 1 - e],
        recv_sem=meta_r.at[me, 1 - e],
        device_id={"exp": 1 - e},
        device_id_type=mesh_id,
    )
    peer.wait_recv()
    peer.wait_send()
    for g in range(heads):
        @pl.when(h + 1 < high)
        def _():
            kv_copy(0, g, h, l).wait_send()

        @pl.loop(1, h + 1)
        def _(t):
            @pl.when(h + 1 < high)
            def _():
                kv_copy(0, g, h - t, l).wait_send()

        for way in range(2):
            for r in range(2):
                context_copy(way, g, p, l, r).wait_send()
        if g == 0:
            context_copy(0, g, p, 1 - l, 0).wait_send()
        else:
            @pl.when(p == 1)
            def _():
                context_copy(0, g, p, 1 - l, 0).wait_send()
                context_copy(1, g, 1 - p, l, 0).wait_send()

        context_copy(1, g, 1 - p, l, 1).wait_send()
    for d, c, half in lower:
        weight_copy((q + d) % squares, half, c, q).wait_send()
        if paired:
            weight_swap((q + d) % squares, half, c).wait_send()
    for p0, l0 in others:
        away(p0, l0, p, l).wait_send()
    for p0, l0 in others + ((p, l),):
        over(p0, l0).wait_send()


def front(keys, values, ids, gates, queries, weight, stream, gain, high, groups):
    whole = pl.BlockSpec(memory_space=pltpu.VMEM)
    away = pl.BlockSpec(memory_space=pl.ANY)
    span, columns = queries.shape
    rows = stream.shape[0]
    features = weight.shape[0]
    heads = keys.shape[1] // HD
    squares = high // 2
    chunks = 4 if features % 128 == 0 else 1
    kind = jnp.bfloat16
    sem = pltpu.SemaphoreType.DMA
    return pl.pallas_call(
        functools.partial(front_kernel, high, groups, chunks),
        out_shape=(
            jax.ShapeDtypeStruct(stream.shape, jnp.float32),
            jax.ShapeDtypeStruct(stream.shape, kind),
            jax.ShapeDtypeStruct((high, LOW, 2, 2 * ids.shape[0], 2 * rows), kind),
        ),
        in_specs=[away, away, whole, whole, away, away, away, whole],
        out_specs=(whole,) * 3,
        scratch_shapes=[
            pltpu.VMEM(queries.shape, kind),
            pltpu.VMEM(stream.shape, kind),
            pltpu.VMEM((heads, high, LOW, span, 2 * HD), kind),
            pltpu.VMEM((squares,) + weight.shape, kind),
            pltpu.VMEM((2, LOW, heads, span, columns // heads), kind),
            pltpu.VMEM((2, LOW, 2, squares, rows, features), kind),
            pltpu.VMEM((2, LOW, squares, rows, features), kind),
            pltpu.VMEM((2, LOW, squares, rows, features), kind),
            pltpu.VMEM((2, LOW, squares, rows, features), kind),
            sem((2 * heads + 3,)),
            sem((high * LOW, 2)),
            sem((high * LOW, 2)),
            sem((2, heads, high, LOW)),
            sem((heads, high, LOW)),
            sem((2, heads, 2, LOW, 2)),
            sem((heads, 2, LOW, 2)),
            sem((squares, 2, chunks)),
            sem((squares, 2, chunks)),
            sem((squares, chunks)),
            sem((2, LOW)),
            sem((2, LOW)),
            sem((2, LOW)),
            sem((2, LOW)),
            pltpu.SemaphoreType.REGULAR,
        ],
        compiler_params=pltpu.CompilerParams(
            collective_id=1, has_side_effects=True, vmem_limit_bytes=VMEM_LIMIT
        ),
        name="front",
    )(keys, values, ids, gates, queries, weight, stream, gain)


def back_kernel(
    high, parts, top, normed_ref, mixed_ref, meta_ref, first_hbm, second_hbm, out_ref,
    choose_ref, combine_ref, every, first, second, picked, act, near, sums, across, running, line,
    local, weight_sem, recv, send, near_s, near_r, across_s, across_r, line_s, line_r
):
    h, l, e = split_position()
    mesh_id = pl.DeviceIdType.MESH
    experts, width, double = first.shape
    hidden = double // 2
    slots = picked.shape[2]
    pairs = high // 2
    span = every.shape[3]
    rows = span // parts
    loads = []
    for i in range(experts):
        loads.append(pltpu.make_async_copy(first_hbm.at[i], first.at[i], weight_sem.at[0, i]))
        loads.append(pltpu.make_async_copy(second_hbm.at[i], second.at[i], weight_sem.at[1, i]))
    for one in loads:
        one.start()
    own = pltpu.make_async_copy(normed_ref, every.at[e, h, l], local.at[0])
    own.start()
    line_barrier(high, h, l, e)
    own.wait()
    device = (h * LOW + l) * 2 + e
    tokens_here, total = combine_ref.shape[2:]

    def build(a, hp):
        meta = jnp.concatenate(
            [
                meta_ref[2 * hp + k, 0, a].astype(jnp.float32) + meta_ref[2 * hp + k, 1, a].astype(jnp.float32)
                for k in range(2)
            ],
            axis=1,
        )
        ids, gates = meta[:top], meta[top:]
        chosen, shares = [], []
        for i in range(experts):
            hit = ids == (device * experts + i).astype(jnp.float32)
            chosen.append(jnp.sum(jnp.where(hit, 1.0, 0.0), axis=0, keepdims=True))
            shares.append(jnp.sum(jnp.where(hit, gates, 0.0), axis=0, keepdims=True))
        line_up = jnp.concatenate(
            chosen + [jnp.zeros_like(chosen[0])] * (-experts % 8), axis=0
        )
        square = (tokens_here, tokens_here)
        row = lax.broadcasted_iota(jnp.int32, square, 0)
        column = lax.broadcasted_iota(jnp.int32, square, 1)
        earlier = jnp.where((row < column) & (row // span == column // span), 1.0, 0.0)
        place = jnp.dot(
            line_up.astype(jnp.bfloat16), earlier.astype(jnp.bfloat16), preferred_element_type=jnp.float32
        )
        tall = (-(-total // 128) * 128, tokens_here)
        number = lax.broadcasted_iota(jnp.int32, tall, 0).astype(jnp.float32)
        block = (lax.broadcasted_iota(jnp.int32, (1, tokens_here), 1) // span).astype(jnp.float32)
        onehot, weigh = jnp.zeros(tall, jnp.float32), jnp.zeros(tall, jnp.float32)
        for i in range(experts):
            match = (number == place[i : i + 1] + block * CAP + i * slots) & (chosen[i] > 0.5)
            onehot = onehot + jnp.where(match, 1.0, 0.0)
            weigh = weigh + jnp.where(match, shares[i], 0.0)
        choose_ref[a, hp] = onehot[:total].astype(choose_ref.dtype)
        combine_ref[a, hp] = jnp.transpose(weigh)[:, :total].astype(combine_ref.dtype)

    def copy(h0, l0, e0, c, way):
        target = (
            {"seq": (h + 1) * LOW + l},
            {"seq": (h - 1) * LOW + l},
            {"seq": h * LOW + 1 - l},
            {"exp": 1 - e},
        )[way]
        ref = every.at[e0, h0, l0, pl.ds(c * rows, rows)]
        return pltpu.make_async_remote_copy(
            src_ref=ref,
            dst_ref=ref,
            send_sem=send.at[way, h0, l0, c],
            recv_sem=recv.at[h0, l0, e0, c],
            device_id=target,
            device_id_type=mesh_id,
        )

    def onward(h0, c, way):
        @pl.when((h + 1 < high) if way == 0 else (h > 0))
        def _():
            copy(h0, l, e, c, way).start()

    def stage(t):
        for c in range(parts):
            for way, h0, fits in ((0, h - t, h - t >= 0), (1, h + t, h + t < high)):
                @pl.when(fits)
                def _():
                    copy(h0, l, e, c, way).wait_recv()
                    onward(h0, c, way)
                    copy(h0, l, e, c, 2).start()
                    copy(h0, l, e, c, 3).start()

    def from_across(t):
        for c in range(parts):
            for h0, fits in ((h - t, h - t >= 0), (h + t, h + t < high))[: 2 if t else 1]:
                @pl.when(fits)
                def _():
                    copy(h0, 1 - l, e, c, 2).wait_recv()
                    copy(h0, 1 - l, e, c, 3).start()

    def from_core(t, l0):
        for c in range(parts):
            for h0, fits in ((h - t, h - t >= 0), (h + t, h + t < high))[: 2 if t else 1]:
                @pl.when(fits)
                def _():
                    copy(h0, l0, 1 - e, c, 3).wait_recv()

    def sent():
        for c in range(parts):
            for h0 in range(high):
                for l0 in range(LOW):
                    copy(h0, l0, e, c, 3).wait_send()
                copy(h0, l, e, c, 2).wait_send()

                @pl.when((h + 1 < high) & (h0 <= h))
                def _():
                    copy(h0, l, e, c, 0).wait_send()

                @pl.when((h > 0) & (h0 >= h))
                def _():
                    copy(h0, l, e, c, 1).wait_send()

    @pl.when(e == 0)
    def _():
        for c in range(parts):
            onward(h, c, 0)
            onward(h, c, 1)
            copy(h, l, e, c, 2).start()
            copy(h, l, e, c, 3).start()

    for hp in range(pairs):
        build(0, hp)

    @pl.when(e == 0)
    def _():
        for t in range(1, high):
            stage(t)
            from_across(t - 1)
        from_across(high - 1)

    @pl.when(e == 1)
    def _():
        for t in range(high):
            from_core(t, l)
            for c in range(parts):
                @pl.when(h == t)
                def _():
                    onward(h, c, 0)

                @pl.when(h + t == high - 1)
                def _():
                    onward(h, c, 1)
        for c in range(parts):
            copy(h, l, e, c, 2).start()
            copy(h, l, e, c, 3).start()
        for t in range(high):
            from_core(t, 1 - l)

    tile = 512

    def pick(a):
        @pl.loop(0, pairs)
        def _(hp):
            for n in range(0, width, tile):
                tokens = every[a, pl.ds(2 * hp, 2), :, :, pl.ds(n, tile)].reshape(tokens_here, tile)
                value = jnp.dot(choose_ref[a, hp], tokens, preferred_element_type=jnp.float32)
                for i in range(experts):
                    picked[i, hp, :, pl.ds(n, tile)] = value[i * slots : (i + 1) * slots].astype(
                        picked.dtype
                    )

    def run_experts(hooks):
        def run(i, carry):
            step = 256
            taken = picked[i].reshape(pairs * slots, width)
            for f in range(0, hidden, step):
                gate = jnp.dot(taken, first[i, :, pl.ds(f, step)], preferred_element_type=jnp.float32)
                up = jnp.dot(
                    taken, first[i, :, pl.ds(hidden + f, step)], preferred_element_type=jnp.float32
                )
                act[:, pl.ds(f, step)] = (gate / (1.0 + jnp.exp(-gate)) * up).astype(act.dtype)
            for n in range(0, width, tile):
                value = jnp.dot(
                    act[...], second[i, :, pl.ds(n, tile)], preferred_element_type=jnp.float32
                ).astype(picked.dtype)
                picked[i, :, :, pl.ds(n, tile)] = value.reshape(pairs, slots, tile)
            for k, hook in hooks:
                @pl.when((e == 1) & (i == min(k, experts - 1)))
                def _():
                    hook()
            return carry

        lax.fori_loop(0, experts, run, 0)

    order = []
    for i in range(high):
        order.append(i // 2 if i % 2 == 0 else high - 1 - i // 2)
    turns = []
    for h0 in order:
        if h0 // 2 not in turns:
            turns.append(h0 // 2)
    shape = (2,) + every.shape[2:4]

    def to_near(h0, l0, c):
        at = pl.ds(c * rows, rows)
        return pltpu.make_async_remote_copy(
            src_ref=every.at[1 - e, h0, l0, at],
            dst_ref=near.at[h0, l0, at],
            send_sem=near_s.at[h0, l0, c],
            recv_sem=near_r.at[h0, l0, c],
            device_id={"exp": 1 - e},
            device_id_type=mesh_id,
        )

    def to_across(h0, c):
        at = pl.ds(c * rows, rows)
        return pltpu.make_async_remote_copy(
            src_ref=sums.at[h0, at],
            dst_ref=across.at[h0, at],
            send_sem=across_s.at[h0, c],
            recv_sem=across_r.at[h0, c],
            device_id={"seq": h * LOW + 1 - l},
            device_id_type=mesh_id,
        )

    def to_line(way, h0, c):
        at = pl.ds(c * rows, rows)
        return pltpu.make_async_remote_copy(
            src_ref=running.at[h0, at],
            dst_ref=line.at[way, h0, at],
            send_sem=line_s.at[way, h0, c],
            recv_sem=line_r.at[way, h0, c],
            device_id={"seq": (h - 1 + 2 * way) * LOW + l},
            device_id_type=mesh_id,
        )

    pieces = [(h0, c) for h0 in order for c in range(parts)]

    def combine(a):
        for hp in turns:
            for n in range(0, width, tile):
                rows_here = jnp.concatenate(
                    [picked[i, hp, :, pl.ds(n, tile)] for i in range(experts)], axis=0
                )
                value = jnp.dot(combine_ref[a, hp], rows_here, preferred_element_type=jnp.float32)
                every[a, 2 * hp : 2 * hp + 2, :, :, pl.ds(n, tile)] = value.astype(every.dtype).reshape(
                    shape + (tile,)
                )

            @pl.when(e != a)
            def _():
                for l0 in (1 - l, l):
                    for h0 in (2 * hp, 2 * hp + 1):
                        for c in range(parts):
                            to_near(h0, l0, c).start()

    def over_y():
        for h0, c in pieces:
            at = pl.ds(c * rows, rows)
            to_near(h0, 1 - l, c).wait_recv()
            value = every[e, h0, 1 - l, at].astype(jnp.float32) + near[h0, 1 - l, at].astype(jnp.float32)
            sums[h0, at] = value.astype(sums.dtype)
            to_across(h0, c).start()

    def along_line():
        for h0, c in pieces:
            at = pl.ds(c * rows, rows)
            to_near(h0, l, c).wait_recv()
            to_across(h0, c).wait_recv()

            def held():
                value = every[e, h0, l, at].astype(jnp.float32) + near[h0, l, at].astype(jnp.float32)
                return value + across[h0, at].astype(jnp.float32)

            @pl.when(h0 < h)
            def _():
                @pl.when(h + 1 < high)
                def _():
                    to_line(0, h0, c).wait_recv()
                    running[h0, at] = (held() + line[0, h0, at].astype(jnp.float32)).astype(running.dtype)

                @pl.when(h + 1 >= high)
                def _():
                    running[h0, at] = held().astype(running.dtype)

                to_line(0, h0, c).start()

            @pl.when(h0 > h)
            def _():
                @pl.when(h > 0)
                def _():
                    to_line(1, h0, c).wait_recv()
                    running[h0, at] = (held() + line[1, h0, at].astype(jnp.float32)).astype(running.dtype)

                @pl.when(h <= 0)
                def _():
                    running[h0, at] = held().astype(running.dtype)

                to_line(1, h0, c).start()

    pick(0)
    for one in loads:
        one.wait()
    last = [(max(0, experts - 2), functools.partial(stage, t)) for t in range(3, high)]
    run_experts(
        [(0, functools.partial(stage, 1)), (0, functools.partial(from_across, 0))]
        + [(1, functools.partial(stage, 2))] * (high > 2)
        + last
        + [(2, functools.partial(from_across, 1))] * (high > 1)
    )

    @pl.when(e == 0)
    def _():
        sent()

    @pl.when(e == 1)
    def _():
        for t in range(2, high - 1):
            from_across(t)

    combine(0)
    for hp in range(pairs):
        build(1, hp)

    @pl.when(e == 1)
    def _():
        for t in range(max(2, high - 1), high):
            from_across(t)

    @pl.when(e == 0)
    def _():
        over_y()
        for l0 in (l, 1 - l):
            for t in range(high):
                from_core(t, l0)

    pick(1)
    run_experts([])

    @pl.when(e == 1)
    def _():
        sent()

    combine(1)

    @pl.when(e == 1)
    def _():
        over_y()

    along_line()
    for c in range(parts):
        at = pl.ds(c * rows, rows)
        value = every[e, h, l, at].astype(jnp.float32) + near[h, l, at].astype(jnp.float32)
        partial = value + across[h, at].astype(jnp.float32) + mixed_ref[at, :]

        @pl.when(h + 1 < high)
        def _():
            to_line(0, h, c).wait_recv()

        @pl.when(h + 1 >= high)
        def _():
            line[0, h, at] = jnp.zeros_like(line[0, h, at])

        @pl.when(h > 0)
        def _():
            to_line(1, h, c).wait_recv()

        @pl.when(h <= 0)
        def _():
            line[1, h, at] = jnp.zeros_like(line[1, h, at])

        value = partial + line[0, h, at].astype(jnp.float32) + line[1, h, at].astype(jnp.float32)
        out_ref[at, :] = value.astype(out_ref.dtype)

    for h0, c in pieces:
        for l0 in range(LOW):
            to_near(h0, l0, c).wait_send()
        to_across(h0, c).wait_send()

        @pl.when(h0 < h)
        def _():
            to_line(0, h0, c).wait_send()

        @pl.when(h0 > h)
        def _():
            to_line(1, h0, c).wait_send()


def back(normed, mixed, meta, expert_in, expert_out, high, top):
    rows, width = mixed.shape
    parts = PARTS
    whole = pl.BlockSpec(memory_space=pltpu.VMEM)
    away = pl.BlockSpec(memory_space=pl.ANY)
    kind = jnp.bfloat16
    sem = pltpu.SemaphoreType.DMA
    experts = expert_in.shape[0]
    slots = LOW * 2 * CAP
    tokens = LOW * 2 * rows
    pairs = high // 2
    return pl.pallas_call(
        functools.partial(back_kernel, high, parts, top),
        out_shape=jax.ShapeDtypeStruct((rows, width), kind),
        in_specs=[whole] * 3 + [away] * 2,
        out_specs=whole,
        scratch_shapes=[
            pltpu.VMEM((2, pairs, experts * slots, tokens), kind),
            pltpu.VMEM((2, pairs, tokens, experts * slots), kind),
            pltpu.VMEM((2, high, LOW, rows, width), kind),
            pltpu.VMEM(expert_in.shape, kind),
            pltpu.VMEM(expert_out.shape, kind),
            pltpu.VMEM((experts, pairs, slots, width), kind),
            pltpu.VMEM((pairs * slots, expert_out.shape[1]), kind),
            pltpu.VMEM((high, LOW, rows, width), kind),
            pltpu.VMEM((high, rows, width), kind),
            pltpu.VMEM((high, rows, width), kind),
            pltpu.VMEM((high, rows, width), kind),
            pltpu.VMEM((2, high, rows, width), kind),
            sem((1,)),
            sem((2, experts)),
            sem((high, LOW, 2, parts)),
            sem((4, high, LOW, parts)),
        ]
        + [sem((high, LOW, parts))] * 2
        + [sem((high, parts))] * 2
        + [sem((2, high, parts))] * 2,
        compiler_params=pltpu.CompilerParams(
            collective_id=2, has_side_effects=True, vmem_limit_bytes=VMEM_LIMIT
        ),
        name="back",
    )(normed, mixed, meta, expert_in, expert_out)


def on_device(
    stream,
    queries,
    key_rows,
    value_rows,
    out_weight,
    norm_gain,
    expert_ids,
    gate_weights,
    expert_in,
    expert_out,
):
    high = lax.axis_size("seq") // LOW
    mixed, normed, meta = front(
        key_rows, value_rows, expert_ids.T, gate_weights.T, queries, out_weight, stream,
        norm_gain.reshape(1, -1), high, lax.axis_size("groups"),
    )
    return back(normed, mixed, meta, expert_in, expert_out, high, expert_ids.shape[1])


def solution(mesh):
    in_specs = (
        P(("groups", "seq", "exp"), None),
        P(("groups", "seq"), "exp"),
        P(("groups", "seq"), "exp"),
        P(("groups", "seq"), "exp"),
        P("seq", "exp"),
        P(),
        P(("groups", "seq", "exp"), None),
        P(("groups", "seq", "exp"), None),
        P(("seq", "exp"), None, None),
        P(("seq", "exp"), None, None),
    )
    out_specs = P(("groups", "seq", "exp"), None)
    return jax.shard_map(
        on_device, mesh=mesh, in_specs=in_specs, out_specs=out_specs, check_vma=False
    )
```

```python
import functools

import jax
import jax.numpy as jnp
from jax import lax
from jax.experimental import pallas as pl
from jax.experimental.pallas import tpu as pltpu
from jax.sharding import PartitionSpec as P

HD = 128
EXPERTS = 64
CAP = 12
LOW = 2
PARTS = 4
VMEM_LIMIT = 67043328
neg_large = -1e30


def split_position():
    seq = lax.axis_index("seq")
    return seq // LOW, seq % LOW, lax.axis_index("exp")


def line_barrier(high, h, l, e):
    barrier = pltpu.get_barrier_semaphore()

    def greet(target):
        pl.semaphore_signal(barrier, inc=1, device_id=target, device_id_type=pl.DeviceIdType.MESH)

    @pl.when(h + 1 < high)
    def _():
        greet({"seq": (h + 1) * LOW + l})

    @pl.when(h > 0)
    def _():
        greet({"seq": (h - 1) * LOW + l})

    greet({"seq": h * LOW + 1 - l})
    greet({"exp": 1 - e})

    ends = jnp.where(h + 1 < high, 1, 0) + jnp.where(h > 0, 1, 0)
    pl.semaphore_wait(barrier, ends + 2)


def whole_barrier(seq, groups):
    barrier = pltpu.get_barrier_semaphore()
    me, e = lax.axis_index("seq"), lax.axis_index("exp")

    def greet(target):
        pl.semaphore_signal(barrier, inc=1, device_id=target, device_id_type=pl.DeviceIdType.MESH)

    greet({"exp": 1 - e})
    for d in range(1, seq):
        for e0 in range(2):
            greet({"seq": (me + d) % seq, "exp": e0})
    count = 2 * seq - 1
    if groups % 2 == 0:
        greet({"groups": flip(lax.axis_index("groups"))})
        count += 1
    pl.semaphore_wait(barrier, count)


def flip(i):
    return i + 1 - 2 * (i % 2)


def attend_piece(q, k, v, state, allowed):
    largest, total, summed = state
    scale = 1.0 / (HD ** 0.5)
    scores = lax.dot_general(
        q, k, (((1,), (1,)), ((), ())), preferred_element_type=jnp.float32
    ) * scale
    if allowed is not None:
        scores = jnp.where(allowed, scores, neg_large)
    new = jnp.maximum(largest, jnp.max(scores, axis=-1, keepdims=True))
    rescale = jnp.exp(largest - new)
    exps = jnp.exp(scores - new)
    total = total * rescale + jnp.sum(exps, axis=-1, keepdims=True)
    summed = summed * rescale + jnp.dot(
        exps.astype(jnp.bfloat16), v, preferred_element_type=jnp.float32
    )
    return new, total, summed


def front_kernel(
    high, groups, chunks, key_in, value_in, ids_ref, gates_ref, query_in, weight_in, stream_in, gain_ref,
    mixed_ref, normed_ref, meta_all,
    query_ref, stream_ref, kv, weights, contexts, part, mine, ready, landed,
    local, meta_s, meta_r, kv_s, kv_r, ctx_s, ctx_r, weight_s, weight_r, swap_s, over_s, over_r,
    away_s, away_r, turn
):
    h, l, e = split_position()
    q, p = h // 2, h % 2
    me, seq = h * LOW + l, high * LOW
    squares = high // 2
    paired = groups % 2 == 0
    x = lax.axis_index("groups") % 2 if paired else 0
    mesh_id = pl.DeviceIdType.MESH
    heads = key_in.shape[1] // HD
    span, columns = query_ref.shape
    per_group = columns // (heads * HD)
    wide = per_group * HD
    top, rows_e = ids_ref.shape
    features = weight_in.shape[0]
    loads = []
    for g in range(heads):
        at = pl.ds(g * HD, HD)
        loads.append(pltpu.make_async_copy(key_in.at[:, at], kv.at[g, h, l, :, pl.ds(0, HD)], local.at[2 * g]))
        loads.append(pltpu.make_async_copy(value_in.at[:, at], kv.at[g, h, l, :, pl.ds(HD, HD)], local.at[2 * g + 1]))
    query_load = pltpu.make_async_copy(query_in, query_ref, local.at[2 * heads])
    weight_load = pltpu.make_async_copy(weight_in, weights.at[q], local.at[2 * heads + 1])
    stream_load = pltpu.make_async_copy(stream_in, stream_ref, local.at[2 * heads + 2])
    for one in loads + [query_load, weight_load, stream_load]:
        one.start()

    @pl.when(l == 0)
    def _():
        for g in range(heads):
            kv[g, h, 1] = jnp.zeros_like(kv[g, h, 1])

    listed = jnp.concatenate([ids_ref[...].astype(jnp.float32), gates_ref[...]], axis=0)
    blank = jnp.zeros_like(listed)
    meta_all[h, l, e] = jnp.where(
        l == 0,
        jnp.concatenate([listed, blank], axis=1),
        jnp.concatenate([blank, listed], axis=1),
    ).astype(meta_all.dtype)
    whole_barrier(seq, groups)

    def kv_copy(way, g, h0, l0):
        ref = kv.at[g, h0, l0]
        target = ({"seq": (h + 1) * LOW + l}, {"seq": h * LOW + 1 - l})[way]
        return pltpu.make_async_remote_copy(
            src_ref=ref,
            dst_ref=ref,
            send_sem=kv_s.at[way, g, h0, l0],
            recv_sem=kv_r.at[g, h0, l0],
            device_id=target,
            device_id_type=mesh_id,
        )

    def meta_copy(d, e0, source):
        s0 = (me + d) % seq
        ref = meta_all.at[h, l, e]
        return pltpu.make_async_remote_copy(
            src_ref=ref,
            dst_ref=ref,
            send_sem=meta_s.at[s0, e0],
            recv_sem=meta_r.at[source[0], source[1]],
            device_id={"seq": s0, "exp": e0},
            device_id_type=mesh_id,
        )

    def weight_rows(half, c):
        step = features // (2 * chunks)
        return pl.ds((half * chunks + c) * step, step)

    def weight_copy(q0, half, c, owner):
        ref = weights.at[owner, weight_rows(half, c)]
        return pltpu.make_async_remote_copy(
            src_ref=ref,
            dst_ref=ref,
            send_sem=weight_s.at[q0, half, c],
            recv_sem=weight_r.at[owner, half, c],
            device_id={"seq": (2 * q0 + p) * LOW + l},
            device_id_type=mesh_id,
        )

    def weight_swap(owner, half, c):
        ref = weights.at[owner, weight_rows(half, c)]
        return pltpu.make_async_remote_copy(
            src_ref=ref,
            dst_ref=ref,
            send_sem=swap_s.at[owner, c],
            recv_sem=weight_r.at[owner, half, c],
            device_id={"groups": flip(lax.axis_index("groups"))},
            device_id_type=mesh_id,
        )

    halves = [x] if paired else [0, 1]
    lower = [(d, c, half) for d in range(1, squares) for c in range(chunks) for half in halves]

    def send_weights(up):
        for d, c, half in lower:
            q0 = (q + d) % squares

            @pl.when((q0 > q) if up else (q0 < q))
            def _():
                weight_copy(q0, half, c, q).start()

    for one in loads:
        one.wait()
    for g in range(heads):
        @pl.when(h + 1 < high)
        def _():
            kv_copy(0, g, h, l).start()

        @pl.when(l == 0)
        def _():
            kv_copy(1, g, h, l).start()
    for d in range(seq):
        for e0 in range(2):
            if d > 0:
                meta_copy(d, e0, (me, e)).start()
    pltpu.make_async_remote_copy(
        src_ref=meta_all.at[h, l, e],
        dst_ref=meta_all.at[h, l, e],
        send_sem=meta_s.at[me, 1 - e],
        recv_sem=meta_r.at[me, e],
        device_id={"exp": 1 - e},
        device_id_type=mesh_id,
    ).start()
    weight_load.wait()
    @pl.when(p == 0)
    def _():
        send_weights(False)

    query_load.wait()

    def half_rows(r):
        step = span // 2
        return pl.ds(r * step, step)

    def context_copy(way, g, p0, l0, r):
        ref = contexts.at[p0, l0, g, half_rows(r)]
        target = ({"seq": (2 * q + 1 - p) * LOW + l}, {"seq": h * LOW + 1 - l})[way]
        return pltpu.make_async_remote_copy(
            src_ref=ref,
            dst_ref=ref,
            send_sem=ctx_s.at[way, g, p0, l0, r],
            recv_sem=ctx_r.at[g, p0, l0, r],
            device_id=target,
            device_id_type=mesh_id,
        )

    queries = [
        jnp.concatenate(
            [query_ref[:, pl.ds((g * per_group + i) * HD, HD)] for i in range(per_group)], axis=0
        )
        for g in range(heads)
    ]

    def attend(h0, states, allowed):
        result = []
        for g in range(heads):
            both = kv[g, h0].reshape(LOW * span, 2 * HD)
            result.append(attend_piece(queries[g], both[:, :HD], both[:, HD:], states[g], allowed))
        return tuple(result)

    def across(h0):
        for g in range(heads):
            kv_copy(1, g, h0, 1 - l).wait_recv()

    def relay(h0):
        for g in range(heads):
            kv_copy(0, g, h0, l).wait_recv()

            @pl.when(h + 1 < high)
            def _():
                kv_copy(0, g, h0, l).start()

            kv_copy(1, g, h0, l).start()

    @pl.when(h > 0)
    def _():
        relay(h - 1)

    @pl.when(l == 1)
    def _():
        across(h)

    stacked = per_group * span
    states = tuple(
        (
            jnp.full((stacked, 1), neg_large, jnp.float32),
            jnp.zeros((stacked, 1), jnp.float32),
            jnp.zeros((stacked, HD), jnp.float32),
        )
        for _ in range(heads)
    )
    row = lax.broadcasted_iota(jnp.int32, (stacked, LOW * span), 0) % span
    column = lax.broadcasted_iota(jnp.int32, (stacked, LOW * span), 1)
    states = attend(h, states, column <= row + l * span)

    def step(t, states):
        @pl.when(t < h)
        def _():
            relay(h - t - 1)

        @pl.when((t == 1) & (p == 1))
        def _():
            send_weights(False)

        across(h - t)
        return attend(h - t, states, None)

    states = lax.fori_loop(1, h + 1, step, states)
    for g in range(heads):
        @pl.when(l == 0)
        def _():
            kv_copy(1, g, h, l).wait_send()

        @pl.loop(1, h + 1)
        def _(t):
            kv_copy(1, g, h - t, l).wait_send()

    pl.semaphore_signal(turn, inc=1, device_id={"exp": 1 - e}, device_id_type=mesh_id)
    pl.semaphore_wait(turn, 1)
    for g in range(heads):
        result = (states[g][2] / states[g][1]).astype(contexts.dtype)
        for i in range(per_group):
            contexts[p, l, g, :, pl.ds(i * HD, HD)] = result[i * span : (i + 1) * span]
        for r in range(2):
            context_copy(1, g, p, l, r).start()
            context_copy(0, g, p, l, 1 - r).start()

    send_weights(True)

    def pass_contexts(g):
        for r in range(2):
            context_copy(1, g, p, 1 - l, r).wait_recv()
            if r == 0 and g == 0:
                context_copy(0, g, p, 1 - l, r).start()
            elif r == 0:
                @pl.when(p == 1)
                def _():
                    context_copy(0, g, p, 1 - l, r).start()

            context_copy(0, g, 1 - p, l, 1 - r).wait_recv()
            if r == 0:
                context_copy(1, g, 1 - p, l, 1 - r).start()
            elif g > 0:
                @pl.when(p == 1)
                def _():
                    context_copy(1, g, 1 - p, l, 1 - r).start()

    def project(d, last):
        owner = (q + d) % squares
        for i in range(2):
            l0 = l if i else 1 - l
            product = None
            for g in range(heads):
                term = lax.dot_general(
                    contexts[:, l0, g].reshape(2 * span, wide),
                    weights[owner, :, pl.ds(g * wide, wide)],
                    (((1,), (1,)), ((), ())),
                    preferred_element_type=jnp.float32,
                )
                product = term if product is None else product + term
            product = product.astype(part.dtype)
            for p0 in range(2):
                for e0 in range(2):
                    start = p0 * span + e0 * rows_e
                    part[p0, l0, e0, owner] = product[start : start + rows_e]
            if last:
                for p0 in range(2):
                    over(p0, l0).start()

    def over(p0, l0):
        return pltpu.make_async_remote_copy(
            src_ref=part.at[p0, l0, 1 - e],
            dst_ref=mine.at[p0, l0],
            send_sem=over_s.at[p0, l0],
            recv_sem=over_r.at[p0, l0],
            device_id={"exp": 1 - e},
            device_id_type=mesh_id,
        )

    def forward(some):
        for d, c, half in some:
            owner = (q + d) % squares
            weight_copy(owner, half, c, owner).wait_recv()
            if paired:
                weight_swap(owner, half, c).start()

    split = len(lower) // 2
    for g in range(heads):
        pass_contexts(g)
        forward(lower[:split] if g == 0 else lower[split:])
    for g in range(heads):
        context_copy(0, g, 1 - p, 1 - l, 0).wait_recv()
        context_copy(1, g, 1 - p, 1 - l, 1).wait_recv()
    project(0, squares == 1)
    for d in range(1, squares):
        for c in range(chunks):
            if paired:
                weight_swap((q + d) % squares, 1 - x, c).wait_recv()
        project(d, d == squares - 1)

    def away(p0, l0, p1, l1):
        return pltpu.make_async_remote_copy(
            src_ref=ready.at[p0, l0],
            dst_ref=landed.at[p1, l1],
            send_sem=away_s.at[p0, l0],
            recv_sem=away_r.at[p1, l1],
            device_id={"seq": (2 * q + p0) * LOW + l0},
            device_id_type=mesh_id,
        )

    others = ((1 - p, 1 - l), (p, 1 - l), (1 - p, l))
    for p0, l0 in others + ((p, l),):
        over(p0, l0).wait_recv()
    for p0, l0 in others:
        total = part[p0, l0, e].astype(jnp.float32) + mine[p0, l0].astype(jnp.float32)
        ready[p0, l0] = total.astype(ready.dtype)
        away(p0, l0, p, l).start()
    landed[p, l] = (part[p, l, e].astype(jnp.float32) + mine[p, l].astype(jnp.float32)).astype(landed.dtype)
    stream_load.wait()
    for p0, l0 in others:
        away(p0, l0, p0, l0).wait_recv()
    squared = None
    for h0 in range(high):
        block = pl.ds(h0 * LOW * features, LOW * features)
        pair = jnp.concatenate([landed[h0 % 2, l0, h0 // 2] for l0 in range(LOW)], axis=1)
        value = stream_ref[:, block].astype(jnp.float32) + pair.astype(jnp.float32)
        mixed_ref[:, block] = value
        term = jnp.sum(value * value, axis=-1, keepdims=True)
        squared = term if squared is None else squared + term
    factor = lax.rsqrt(squared / (high * LOW * features) + 1e-06)
    for h0 in range(high):
        block = pl.ds(h0 * LOW * features, LOW * features)
        normed_ref[:, block] = (mixed_ref[:, block] * factor * gain_ref[:, block]).astype(
            normed_ref.dtype
        )

    for d in range(seq):
        for e0 in range(2):
            if d > 0:
                meta_copy(d, e0, ((me + d) % seq, e0)).wait_recv()
                meta_copy(d, e0, (me, e)).wait_send()
    peer = pltpu.make_async_remote_copy(
        src_ref=meta_all.at[h, l, e],
        dst_ref=meta_all.at[h, l, e],
        send_sem=meta_s.at[me, 1 - e],
        recv_sem=meta_r.at[me, 1 - e],
        device_id={"exp": 1 - e},
        device_id_type=mesh_id,
    )
    peer.wait_recv()
    peer.wait_send()
    for g in range(heads):
        @pl.when(h + 1 < high)
        def _():
            kv_copy(0, g, h, l).wait_send()

        @pl.loop(1, h + 1)
        def _(t):
            @pl.when(h + 1 < high)
            def _():
                kv_copy(0, g, h - t, l).wait_send()

        for way in range(2):
            for r in range(2):
                context_copy(way, g, p, l, r).wait_send()
        if g == 0:
            context_copy(0, g, p, 1 - l, 0).wait_send()
        else:
            @pl.when(p == 1)
            def _():
                context_copy(0, g, p, 1 - l, 0).wait_send()
                context_copy(1, g, 1 - p, l, 0).wait_send()

        context_copy(1, g, 1 - p, l, 1).wait_send()
    for d, c, half in lower:
        weight_copy((q + d) % squares, half, c, q).wait_send()
        if paired:
            weight_swap((q + d) % squares, half, c).wait_send()
    for p0, l0 in others:
        away(p0, l0, p, l).wait_send()
    for p0, l0 in others + ((p, l),):
        over(p0, l0).wait_send()


def front(keys, values, ids, gates, queries, weight, stream, gain, high, groups):
    whole = pl.BlockSpec(memory_space=pltpu.VMEM)
    away = pl.BlockSpec(memory_space=pl.ANY)
    span, columns = queries.shape
    rows = stream.shape[0]
    features = weight.shape[0]
    heads = keys.shape[1] // HD
    squares = high // 2
    chunks = 4 if features % 128 == 0 else 1
    kind = jnp.bfloat16
    sem = pltpu.SemaphoreType.DMA
    return pl.pallas_call(
        functools.partial(front_kernel, high, groups, chunks),
        out_shape=(
            jax.ShapeDtypeStruct(stream.shape, jnp.float32),
            jax.ShapeDtypeStruct(stream.shape, kind),
            jax.ShapeDtypeStruct((high, LOW, 2, 2 * ids.shape[0], 2 * rows), kind),
        ),
        in_specs=[away, away, whole, whole, away, away, away, whole],
        out_specs=(whole,) * 3,
        scratch_shapes=[
            pltpu.VMEM(queries.shape, kind),
            pltpu.VMEM(stream.shape, kind),
            pltpu.VMEM((heads, high, LOW, span, 2 * HD), kind),
            pltpu.VMEM((squares,) + weight.shape, kind),
            pltpu.VMEM((2, LOW, heads, span, columns // heads), kind),
            pltpu.VMEM((2, LOW, 2, squares, rows, features), kind),
            pltpu.VMEM((2, LOW, squares, rows, features), kind),
            pltpu.VMEM((2, LOW, squares, rows, features), kind),
            pltpu.VMEM((2, LOW, squares, rows, features), kind),
            sem((2 * heads + 3,)),
            sem((high * LOW, 2)),
            sem((high * LOW, 2)),
            sem((2, heads, high, LOW)),
            sem((heads, high, LOW)),
            sem((2, heads, 2, LOW, 2)),
            sem((heads, 2, LOW, 2)),
            sem((squares, 2, chunks)),
            sem((squares, 2, chunks)),
            sem((squares, chunks)),
            sem((2, LOW)),
            sem((2, LOW)),
            sem((2, LOW)),
            sem((2, LOW)),
            pltpu.SemaphoreType.REGULAR,
        ],
        compiler_params=pltpu.CompilerParams(
            collective_id=1, has_side_effects=True, vmem_limit_bytes=VMEM_LIMIT
        ),
        name="front",
    )(keys, values, ids, gates, queries, weight, stream, gain)


def back_kernel(
    high, top, normed_ref, mixed_ref, meta_ref, first_hbm, second_hbm, out_ref,
    choose_ref, combine_ref, every, first, second, picked, act, near, sums, across, running, line,
    ours, given, local, weight_sem, recv, send, near_s, near_r, across_s, across_r, line_s, line_r,
    last_s, last_r
):
    h, l, e = split_position()
    mesh_id = pl.DeviceIdType.MESH
    experts, width, double = first.shape
    hidden = double // 2
    slots = picked.shape[2]
    pairs = high // 2
    parts, rows = every.shape[3:5]
    half = parts // 2
    span = parts * rows
    loads = []
    for i in range(experts):
        loads.append(pltpu.make_async_copy(first_hbm.at[i], first.at[i], weight_sem.at[0, i]))
        loads.append(pltpu.make_async_copy(second_hbm.at[i], second.at[i], weight_sem.at[1, i]))
    owns = [
        pltpu.make_async_copy(normed_ref.at[pl.ds(c * rows, rows)], every.at[e, h, l, c], local.at[c])
        for c in range(parts)
    ]
    for one in owns + loads:
        one.start()
    line_barrier(high, h, l, e)
    for one in owns:
        one.wait()
    device = (h * LOW + l) * 2 + e
    tokens_here, total = combine_ref.shape[2:]

    def build(a, hp):
        meta = jnp.concatenate(
            [
                meta_ref[2 * hp + k, 0, a].astype(jnp.float32) + meta_ref[2 * hp + k, 1, a].astype(jnp.float32)
                for k in range(2)
            ],
            axis=1,
        )
        ids, gates = meta[:top], meta[top:]
        chosen, shares = [], []
        for i in range(experts):
            hit = ids == (device * experts + i).astype(jnp.float32)
            chosen.append(jnp.sum(jnp.where(hit, 1.0, 0.0), axis=0, keepdims=True))
            shares.append(jnp.sum(jnp.where(hit, gates, 0.0), axis=0, keepdims=True))
        line_up = jnp.concatenate(
            chosen + [jnp.zeros_like(chosen[0])] * (-experts % 8), axis=0
        )
        square = (tokens_here, tokens_here)
        row = lax.broadcasted_iota(jnp.int32, square, 0)
        column = lax.broadcasted_iota(jnp.int32, square, 1)
        earlier = jnp.where((row < column) & (row // span == column // span), 1.0, 0.0)
        place = jnp.dot(
            line_up.astype(jnp.bfloat16), earlier.astype(jnp.bfloat16), preferred_element_type=jnp.float32
        )
        tall = (-(-total // 128) * 128, tokens_here)
        number = lax.broadcasted_iota(jnp.int32, tall, 0).astype(jnp.float32)
        block = (lax.broadcasted_iota(jnp.int32, (1, tokens_here), 1) // span).astype(jnp.float32)
        onehot, weigh = jnp.zeros(tall, jnp.float32), jnp.zeros(tall, jnp.float32)
        for i in range(experts):
            match = (number == place[i : i + 1] + block * CAP + i * slots) & (chosen[i] > 0.5)
            onehot = onehot + jnp.where(match, 1.0, 0.0)
            weigh = weigh + jnp.where(match, shares[i], 0.0)
        choose_ref[a, hp] = onehot[:total].astype(choose_ref.dtype)
        combine_ref[a, hp] = jnp.transpose(weigh)[:, :total].astype(combine_ref.dtype)

    mine = [e * half + j for j in range(half)]
    theirs = [(1 - e) * half + j for j in range(half)]

    def copy(a, h0, l0, c, way):
        target = (
            {"seq": (h + 1) * LOW + l},
            {"seq": (h - 1) * LOW + l},
            {"seq": h * LOW + 1 - l},
            {"exp": 1 - e},
        )[way]
        ref = every.at[a, h0, l0, c]
        return pltpu.make_async_remote_copy(
            src_ref=ref,
            dst_ref=ref,
            send_sem=send.at[way, a, h0, l0, c],
            recv_sem=recv.at[a, h0, l0, c],
            device_id=target,
            device_id_type=mesh_id,
        )

    def onward(a, h0, c, way):
        @pl.when((h + 1 < high) if way == 0 else (h > 0))
        def _():
            copy(a, h0, l, c, way).start()

    def own_z(a, way):
        for c in mine:
            onward(a, h, c, way)

    def at_distance(t):
        return ((0, h - t, h - t >= 0), (1, h + t, h + t < high))[: 2 if t else 1]

    def stage(a, t, z=True, y=True):
        for c in mine:
            for way, h0, fits in at_distance(t):
                @pl.when(fits)
                def _():
                    if z and t:
                        copy(a, h0, l, c, way).wait_recv()
                        onward(a, h0, c, way)
                    if y:
                        copy(a, h0, l, c, 2).start()
                        if t:
                            copy(a, h0, l, c, 3).start()

    def from_across(a, t):
        for c in mine:
            for _, h0, fits in at_distance(t):
                @pl.when(fits)
                def _():
                    copy(a, h0, 1 - l, c, 2).wait_recv()
                    copy(a, h0, 1 - l, c, 3).start()

    def swapped(a):
        @pl.when(e != a)
        def _():
            for c in mine:
                copy(a, h, l, c, 3).wait_recv()

    def from_core(a):
        for c in theirs:
            for h0 in range(high):
                @pl.when((h0 != h) | (e != a))
                def _():
                    copy(a, h0, l, c, 3).wait_recv()

                copy(a, h0, 1 - l, c, 3).wait_recv()

    def sent(a):
        @pl.when(e == a)
        def _():
            for c in theirs:
                copy(a, h, l, c, 3).wait_send()

        for c in mine:
            for h0 in range(high):
                @pl.when((h0 != h) | (e == a))
                def _():
                    copy(a, h0, l, c, 3).wait_send()

                copy(a, h0, 1 - l, c, 3).wait_send()
                copy(a, h0, l, c, 2).wait_send()

                @pl.when((h + 1 < high) & (h0 <= h))
                def _():
                    copy(a, h0, l, c, 0).wait_send()

                @pl.when((h > 0) & (h0 >= h))
                def _():
                    copy(a, h0, l, c, 1).wait_send()

    for c in theirs + mine:
        copy(e, h, l, c, 3).start()
    swapped(0)
    own_z(0, 0)
    own_z(0, 1)
    stage(0, 0)
    for hp in range(pairs):
        build(0, hp)
    swapped(1)

    def follow(t):
        @pl.when(h == t)
        def _():
            own_z(1, 0)

        @pl.when(h + t == high - 1)
        def _():
            own_z(1, 1)

    follow(0)
    for t in range(1, high):
        stage(0, t)
        follow(t)
        from_across(0, t - 1)
    stage(1, 0)
    stage(1, 1, y=False)
    from_across(0, high - 1)
    stage(1, 1, z=False)
    from_core(0)
    tile = 512

    def pick(a):
        @pl.loop(0, pairs)
        def _(hp):
            for n in range(0, width, tile):
                tokens = every[a, pl.ds(2 * hp, 2), :, :, :, pl.ds(n, tile)].reshape(tokens_here, tile)
                value = jnp.dot(choose_ref[a, hp], tokens, preferred_element_type=jnp.float32)
                for i in range(experts):
                    picked[i, hp, :, pl.ds(n, tile)] = value[i * slots : (i + 1) * slots].astype(
                        picked.dtype
                    )

    def run_experts(hooks):
        def run(i, carry):
            step = 256
            taken = picked[i].reshape(pairs * slots, width)
            for f in range(0, hidden, step):
                gate = jnp.dot(taken, first[i, :, pl.ds(f, step)], preferred_element_type=jnp.float32)
                up = jnp.dot(
                    taken, first[i, :, pl.ds(hidden + f, step)], preferred_element_type=jnp.float32
                )
                act[:, pl.ds(f, step)] = (gate / (1.0 + jnp.exp(-gate)) * up).astype(act.dtype)
            for n in range(0, width, tile):
                value = jnp.dot(
                    act[...], second[i, :, pl.ds(n, tile)], preferred_element_type=jnp.float32
                ).astype(picked.dtype)
                picked[i, :, :, pl.ds(n, tile)] = value.reshape(pairs, slots, tile)
            for k, hook in hooks:
                @pl.when(i == min(k, experts - 1))
                def _():
                    hook()
            return carry

        lax.fori_loop(0, experts, run, 0)

    turns = [jnp.where(2 * h >= high, k, pairs - 1 - k) for k in range(pairs)]

    def far_first(act_on):
        for d in range(high - 1, -1, -1):
            for _, h0, fits in at_distance(d):
                @pl.when(fits)
                def _():
                    act_on(h0)

    shape = (2,) + every.shape[2:5]

    def to_near(a, h0, l0, j):
        return pltpu.make_async_remote_copy(
            src_ref=every.at[a, h0, l0, theirs[j]],
            dst_ref=near.at[a, h0, l0, j],
            send_sem=near_s.at[a, h0, l0, j],
            recv_sem=near_r.at[a, h0, l0, j],
            device_id={"exp": 1 - e},
            device_id_type=mesh_id,
        )

    def to_across(a, h0, j):
        return pltpu.make_async_remote_copy(
            src_ref=sums.at[a, h0, j],
            dst_ref=across.at[a, h0, j],
            send_sem=across_s.at[a, h0, j],
            recv_sem=across_r.at[a, h0, j],
            device_id={"seq": h * LOW + 1 - l},
            device_id_type=mesh_id,
        )

    def to_line(way, a, h0, j):
        return pltpu.make_async_remote_copy(
            src_ref=running.at[a, h0, j],
            dst_ref=line.at[way, a, h0, j],
            send_sem=line_s.at[way, a, h0, j],
            recv_sem=line_r.at[way, a, h0, j],
            device_id={"seq": (h - 1 + 2 * way) * LOW + l},
            device_id_type=mesh_id,
        )

    def to_other(j):
        return pltpu.make_async_remote_copy(
            src_ref=ours.at[j],
            dst_ref=given.at[j],
            send_sem=last_s.at[j],
            recv_sem=last_r.at[j],
            device_id={"exp": 1 - e},
            device_id_type=mesh_id,
        )

    def combine(a):
        for hp in turns:
            for n in range(0, width, tile):
                rows_here = jnp.concatenate(
                    [picked[i, hp, :, pl.ds(n, tile)] for i in range(experts)], axis=0
                )
                value = jnp.dot(combine_ref[a, hp], rows_here, preferred_element_type=jnp.float32)
                every[a, pl.ds(2 * hp, 2), :, :, :, pl.ds(n, tile)] = value.astype(
                    every.dtype
                ).reshape(shape + (tile,))
            for l0 in (1 - l, l):
                for h0 in (2 * hp, 2 * hp + 1):
                    for j in range(half):
                        to_near(a, h0, l0, j).start()

    def pair_sum(a, h0, l0, j):
        return every[a, h0, l0, mine[j]].astype(jnp.float32) + near[a, h0, l0, j].astype(jnp.float32)

    def over_y(a):
        def one(h0):
            for j in range(half):
                to_near(a, h0, 1 - l, j).wait_recv()
                sums[a, h0, j] = pair_sum(a, h0, 1 - l, j).astype(sums.dtype)
                to_across(a, h0, j).start()

        far_first(one)

    def held(a, h0, j):
        return pair_sum(a, h0, l, j) + across[a, h0, j].astype(jnp.float32)

    def ready(a, h0, j):
        to_near(a, h0, l, j).wait_recv()
        to_across(a, h0, j).wait_recv()

    def hand_on(a, h0, j):
        ready(a, h0, j)
        for way, fits, first_here in ((0, h0 < h, h + 1 >= high), (1, h0 > h, h <= 0)):
            @pl.when(fits)
            def _():
                @pl.when(jnp.logical_not(first_here))
                def _():
                    to_line(way, a, h0, j).wait_recv()
                    running[a, h0, j] = (
                        held(a, h0, j) + line[way, a, h0, j].astype(jnp.float32)
                    ).astype(running.dtype)

                @pl.when(first_here)
                def _():
                    running[a, h0, j] = held(a, h0, j).astype(running.dtype)

                to_line(way, a, h0, j).start()

    def wave(a, k):
        def one(h0):
            @pl.when(((h0 < h) & (h + k == high - 1)) | ((h0 > h) & (h == k)))
            def _():
                for j in range(half):
                    hand_on(a, h0, j)

        far_first(one)

    def arrived(a, j):
        value = held(a, h, j)

        @pl.when(h + 1 < high)
        def _():
            to_line(0, a, h, j).wait_recv()

        @pl.when(h + 1 >= high)
        def _():
            line[0, a, h, j] = jnp.zeros_like(line[0, a, h, j])

        @pl.when(h > 0)
        def _():
            to_line(1, a, h, j).wait_recv()

        @pl.when(h <= 0)
        def _():
            line[1, a, h, j] = jnp.zeros_like(line[1, a, h, j])

        return value + line[0, a, h, j].astype(jnp.float32) + line[1, a, h, j].astype(jnp.float32)

    pick(0)
    for one in loads:
        one.wait()
    def later():
        for t in range(3, high):
            stage(1, t)

    hooks = [(0, functools.partial(stage, 1, 2))] if high > 2 else []
    hooks += [(1, functools.partial(from_across, 1, 0)), (2, later), (2, functools.partial(from_across, 1, 1))]
    run_experts(hooks)
    for t in range(2, high - 1):
        from_across(1, t)
    sent(0)
    combine(0)
    for hp in range(pairs):
        build(1, hp)
    for t in range(max(2, high - 1), high):
        from_across(1, t)
    over_y(0)
    from_core(1)
    pick(1)
    run_experts([])
    sent(1)
    combine(1)
    wave(0, 0)
    over_y(1)
    for k in range(1, high - 1):
        wave(0, k)

    def pass_on(h0):
        for j in range(half):
            hand_on(1, h0, j)

    far_first(pass_on)
    for j in range(half):
        ready(0, h, j)
    for j in range(half):
        ours[j] = arrived(1 - e, j).astype(ours.dtype)
        to_other(j).start()

    def rows_of(c):
        return pl.ds(pl.multiple_of(c * rows, rows), rows)

    for j in range(half):
        at = rows_of(mine[j])
        out_ref[at, :] = (arrived(e, j) + mixed_ref[at, :]).astype(out_ref.dtype)
    for j in range(half):
        at = rows_of(theirs[j])
        to_other(j).wait_recv()
        out_ref[at, :] = (given[j].astype(jnp.float32) + mixed_ref[at, :]).astype(out_ref.dtype)
    for a in range(2):
        for h0 in range(high):
            for j in range(half):
                for l0 in range(LOW):
                    to_near(a, h0, l0, j).wait_send()
                to_across(a, h0, j).wait_send()

                @pl.when(h0 < h)
                def _():
                    to_line(0, a, h0, j).wait_send()

                @pl.when(h0 > h)
                def _():
                    to_line(1, a, h0, j).wait_send()
    for j in range(half):
        to_other(j).wait_send()


def back(normed, mixed, meta, expert_in, expert_out, high, top):
    rows, width = mixed.shape
    parts = PARTS
    half, piece = parts // 2, rows // parts
    whole = pl.BlockSpec(memory_space=pltpu.VMEM)
    away = pl.BlockSpec(memory_space=pl.ANY)
    kind = jnp.bfloat16
    sem = pltpu.SemaphoreType.DMA
    experts = expert_in.shape[0]
    slots = LOW * 2 * CAP
    tokens = LOW * 2 * rows
    pairs = high // 2
    return pl.pallas_call(
        functools.partial(back_kernel, high, top),
        out_shape=jax.ShapeDtypeStruct((rows, width), kind),
        in_specs=[whole] * 3 + [away] * 2,
        out_specs=whole,
        scratch_shapes=[
            pltpu.VMEM((2, pairs, experts * slots, tokens), kind),
            pltpu.VMEM((2, pairs, tokens, experts * slots), kind),
            pltpu.VMEM((2, high, LOW, parts, piece, width), kind),
            pltpu.VMEM(expert_in.shape, kind),
            pltpu.VMEM(expert_out.shape, kind),
            pltpu.VMEM((experts, pairs, slots, width), kind),
            pltpu.VMEM((pairs * slots, expert_out.shape[1]), kind),
            pltpu.VMEM((2, high, LOW, half, piece, width), kind),
            pltpu.VMEM((2, high, half, piece, width), kind),
            pltpu.VMEM((2, high, half, piece, width), kind),
            pltpu.VMEM((2, high, half, piece, width), kind),
            pltpu.VMEM((2, 2, high, half, piece, width), kind),
            pltpu.VMEM((half, piece, width), kind),
            pltpu.VMEM((half, piece, width), kind),
            sem((parts,)),
            sem((2, experts)),
            sem((2, high, LOW, parts)),
            sem((4, 2, high, LOW, parts)),
        ]
        + [sem((2, high, LOW, half))] * 2
        + [sem((2, high, half))] * 2
        + [sem((2, 2, high, half))] * 2
        + [sem((half,))] * 2,
        compiler_params=pltpu.CompilerParams(
            collective_id=2, has_side_effects=True, vmem_limit_bytes=VMEM_LIMIT
        ),
        name="back",
    )(normed, mixed, meta, expert_in, expert_out)


def on_device(
    stream,
    queries,
    key_rows,
    value_rows,
    out_weight,
    norm_gain,
    expert_ids,
    gate_weights,
    expert_in,
    expert_out,
):
    high = lax.axis_size("seq") // LOW
    mixed, normed, meta = front(
        key_rows, value_rows, expert_ids.T, gate_weights.T, queries, out_weight, stream,
        norm_gain.reshape(1, -1), high, lax.axis_size("groups"),
    )
    return back(normed, mixed, meta, expert_in, expert_out, high, expert_ids.shape[1])


def solution(mesh):
    in_specs = (
        P(("groups", "seq", "exp"), None),
        P(("groups", "seq"), "exp"),
        P(("groups", "seq"), "exp"),
        P(("groups", "seq"), "exp"),
        P("seq", "exp"),
        P(),
        P(("groups", "seq", "exp"), None),
        P(("groups", "seq", "exp"), None),
        P(("seq", "exp"), None, None),
        P(("seq", "exp"), None, None),
    )
    out_specs = P(("groups", "seq", "exp"), None)
    return jax.shard_map(
        on_device, mesh=mesh, in_specs=in_specs, out_specs=out_specs, check_vma=False
    )
```
